32 devices in a mesh: section: 2 (over core), tensor: 4 (over y, x), context: 4 (over z).
Axes of the slice: x: 2, y: 2, z: 4, core: 2. Of those that a mesh axis runs over, the one named last changes fastest.
Arguments:
- layer_input: bfloat16 [2, 512, 1024], P(None, 'context'), may hold values from -48 to 48
- out_cotangent: bfloat16 [2, 512, 1024], P(None, 'context'), may hold values from -6 to 6
- seq_lengths: int32 [2, 3], replicated, may hold values from 1 to 256, 512 in all within a row
- block_order: int32 [2, 8], replicated, may hold values from 0 to 7, each once within a row
- ln1_gain: bfloat16 [2, 1024], P('section', 'context'), may hold values from 0.25 to 1.75
- ln1_bias: bfloat16 [2, 1024], P('section', 'context'), may hold values from -4 to 4
- ln2_gain: bfloat16 [2, 1024], P('section', 'context'), may hold values from 0.25 to 1.75
- ln2_bias: bfloat16 [2, 1024], P('section', 'context'), may hold values from -4 to 4
- qkv_weight: bfloat16 [2, 3, 1024, 1024], P('section', None, 'context', 'tensor'), may hold values from -2 to 2
- qkv_bias: bfloat16 [2, 3, 1024], P('section', None, ('tensor', 'context')), may hold values from -4 to 4
- dense_weight: bfloat16 [2, 1024, 1024], P('section', 'tensor', 'context'), may hold values from -1.5 to 1.5
- dense_bias: bfloat16 [2, 1024], P('section', 'context'), may hold values from -4 to 4
- up_weight: bfloat16 [2, 1024, 4096], P('section', 'context', 'tensor'), may hold values from -0.1875 to 0.1875
- up_bias: bfloat16 [2, 4096], P('section', ('tensor', 'context')), may hold values from -4 to 4
- down_weight: bfloat16 [2, 4096, 1024], P('section', 'tensor', 'context'), may hold values from -0.09375 to 0.09375
- down_bias: bfloat16 [2, 1024], P('section', 'context'), may hold values from -4 to 4
Outputs:
- layer_out: bfloat16 [2, 2, 512, 1024], P('section', None, 'context')
- input_grad: bfloat16 [2, 2, 512, 1024], P('section', None, 'context')
- ln1_gain_grad: float32 [2, 1024], P('section', 'context')
- ln1_bias_grad: float32 [2, 1024], P('section', 'context')
- ln2_gain_grad: float32 [2, 1024], P('section', 'context')
- ln2_bias_grad: float32 [2, 1024], P('section', 'context')
- qkv_weight_grad: float32 [2, 3, 1024, 1024], P('section', None, 'context', 'tensor')
- qkv_bias_grad: float32 [2, 3, 1024], P('section', None, ('tensor', 'context'))
- dense_weight_grad: float32 [2, 1024, 1024], P('section', 'tensor', 'context')
- dense_bias_grad: float32 [2, 1024], P('section', 'context')
- up_weight_grad: float32 [2, 1024, 4096], P('section', 'context', 'tensor')
- up_bias_grad: float32 [2, 4096], P('section', ('tensor', 'context'))
- down_weight_grad: float32 [2, 4096, 1024], P('section', 'tensor', 'context')
- down_bias_grad: float32 [2, 1024], P('section', 'context')
The draws below stay inside these ranges and needn't reach their ends.
Inputs may be any that keep to these rules, and one draw needn't show every extreme that they name: `seq_lengths`: row m holds the lengths of the 3 sequences packed one after another into the 512 packed positions of micro-batch m; each row sums to 512 and its largest entry is 256. Each row is a permutation: stored block b of micro-batch m (rows b * 64 to b * 64 + 63) holds packed positions block_order[m, b] * 64 onward in order.
All inputs are finite; a program needn't handle non-finite values.
Results may differ from the reference program's by a relative error of at most 0.03.
The reference program's roundings to bfloat16 on the way count: a program that leaves them out, or rounds other values in their place, can miss the bound.
Values may be sent and summed in bfloat16 or wider, within the bound.
A program may use at most 128 MiB of HBM per device.

```python
import math
import jax
import jax.numpy as jnp
import numpy as np
from jax import lax

D = 1024
H = 16
HD = 64
ROT = 16
FF = 4096
MICRO = 2
SEQ_TOK = 512
MAX_LEN = 256
NSEQ = 3
BLK = 64
NBLK = 8
N_SECTION = 2


def draw_layer_input(key, part):
    subkeys = jax.random.split(key, 3)
    full_shape = (MICRO, SEQ_TOK, D)
    col_scale = jnp.exp(jax.random.uniform(subkeys[1], (1, 1, D), minval=math.log(0.4), maxval=math.log(2.5)))
    row_scale = jnp.exp(jax.random.uniform(subkeys[0], (MICRO, SEQ_TOK, 1), minval=math.log(0.5), maxval=math.log(5.0)))
    noise = jnp.clip(jax.random.normal(subkeys[2], full_shape), -4.0, 4.0)
    values = noise * row_scale * col_scale
    return jnp.clip(values, -48.0, 48.0).astype(jnp.bfloat16)


def draw_qkv_weight(key, part):
    full_shape = (2, 3, D, H * HD)
    spread = 1.0 / math.sqrt(D)
    values = jnp.clip(jax.random.normal(key, full_shape), -6.0, 6.0) * spread
    return values.astype(jnp.bfloat16)


def levels(rng, shape, pieces, smallest, largest):
    loudness, own = 1.0, jax.random.fold_in(rng, 6)
    for dim, blocks in pieces:
        draws = jnp.exp(jax.random.uniform(jax.random.fold_in(own, dim), (blocks,), jnp.float32, smallest / len(pieces), largest / len(pieces)))
        loudness = loudness * jnp.repeat(draws, shape[dim] // blocks).reshape([-1 if axis == dim else 1 for axis in range(len(shape))])
    return loudness


def length_profile(amount, total, bound, slope):
    loads = [(1 << 20) // math.isqrt(standing ** slope) + 1 for standing in range(2, amount + 1)]
    rest, counts = total - bound - (amount - 1), [1] * (amount - 1)
    while rest > 0:
        movable = [i for i in range(amount - 1) if counts[i] < bound]
        mass, remaining = sum([loads[i] for i in movable]), rest
        for i in movable:
            extra = min(bound - counts[i], max(1, remaining * loads[i] // mass), rest)
            counts[i] = counts[i] + extra
            rest = rest - extra
    return np.array([bound] + counts)


def ragged(rng, count, total, limit, skew):
    if count == 2:
        one = jax.random.randint(rng, (), max(1, total - limit), min(limit, total - 1) + 1)
        return jnp.stack([one, total - one])
    sizes = jnp.asarray(length_profile(count, total, limit, skew), jnp.int32)
    couples = (count - 1) // 2
    giver, sink = sizes[1:1 + 2 * couples:2], sizes[2:2 + 2 * couples:2]
    margin = jnp.minimum(giver - 1, limit - sink)
    shifted = jax.random.randint(jax.random.fold_in(rng, 1), (couples,), 0, 1 << 20) % (margin + 1)
    sizes = sizes.at[1:1 + 2 * couples:2].set(giver - shifted).at[2:2 + 2 * couples:2].set(sink + shifted)
    return sizes[jax.random.permutation(jax.random.fold_in(rng, 2), count)]


def gaussian(own_key, extent, scale, reach, shards=(), kind=jnp.bfloat16):
    result = scale * jax.random.normal(own_key, extent, jnp.float32)
    if shards:
        result = result * levels(own_key, extent, shards, -0.22, 0.18)
    return jnp.clip(result, -reach, reach).astype(kind)


def setup_inputs(seed: int = 0) -> dict:
    key_of = jax.random.split(jax.random.key(seed), 17)
    layer_input = draw_layer_input(jax.random.fold_in(key_of[16], 71), 0)
    out_cotangent = gaussian(key_of[1], (MICRO, SEQ_TOK, D), 1.0, 6.0, ((1, 4),))
    seq_lengths = jax.vmap(lambda own: ragged(own, NSEQ, SEQ_TOK, MAX_LEN, 2))(jax.random.split(key_of[2], MICRO)).reshape((MICRO, NSEQ)).astype(jnp.int32)
    block_order = jax.vmap(lambda own: jax.random.permutation(own, NBLK))(jax.random.split(key_of[3], MICRO)).reshape((MICRO, NBLK)).astype(jnp.int32)
    ln1_gain = jnp.clip(1.0 + 0.15 * jax.random.normal(key_of[4], (N_SECTION, D), jnp.float32), 0.25, 1.75).astype(jnp.bfloat16)
    ln1_bias = gaussian(key_of[5], (N_SECTION, D), 0.3, 4.0, ((0, 2), (1, 4)))
    ln2_gain = jnp.clip(1.0 + 0.15 * jax.random.normal(key_of[6], (N_SECTION, D), jnp.float32), 0.25, 1.75).astype(jnp.bfloat16)
    ln2_bias = gaussian(key_of[7], (N_SECTION, D), 0.3, 4.0, ((0, 2), (1, 4)))
    qkv_weight = draw_qkv_weight(jax.random.fold_in(key_of[16], 71), 0)
    qkv_bias = gaussian(key_of[9], (N_SECTION, 3, H * HD), 0.5, 4.0, ((0, 2), (2, 16)))
    dense_weight = gaussian(key_of[10], (N_SECTION, H * HD, D), (HD // 4) ** -0.5, 1.5, ((0, 2), (1, 4), (2, 4)))
    dense_bias = gaussian(key_of[11], (N_SECTION, D), 0.3, 4.0, ((0, 2), (1, 4)))
    up_weight = gaussian(key_of[12], (N_SECTION, D, FF), D ** -0.5, 0.1875, ((0, 2), (1, 4), (2, 4)))
    up_bias = gaussian(key_of[13], (N_SECTION, FF), 0.5, 4.0, ((0, 2), (1, 16)))
    down_weight = gaussian(key_of[14], (N_SECTION, FF, D), FF ** -0.5, 0.09375, ((0, 2), (1, 4), (2, 4)))
    down_bias = gaussian(key_of[15], (N_SECTION, D), 0.3, 4.0, ((0, 2), (1, 4)))
    return dict(layer_input=layer_input, out_cotangent=out_cotangent, seq_lengths=seq_lengths, block_order=block_order, ln1_gain=ln1_gain, ln1_bias=ln1_bias, ln2_gain=ln2_gain, ln2_bias=ln2_bias, qkv_weight=qkv_weight, qkv_bias=qkv_bias, dense_weight=dense_weight, dense_bias=dense_bias, up_weight=up_weight, up_bias=up_bias, down_weight=down_weight, down_bias=down_bias)


EPSILON = 1e-05
MASKED = -1e+30

def packed_layout(lengths, block_perm, block_rows):
    total_rows = block_perm.shape[0] * block_rows
    row_index = jnp.arange(total_rows, dtype=jnp.int32)
    chosen = (row_index // block_rows)[:, None] == jnp.arange(block_perm.shape[0], dtype=jnp.int32)[None, :]
    packed_pos = lax.optimization_barrier(jnp.sum(jnp.where(chosen, block_perm[None, :], 0), axis=1)).astype(jnp.int32) * block_rows + row_index % block_rows
    seq_ends = jnp.cumsum(lengths).astype(jnp.int32)
    passed = seq_ends[None, :] <= packed_pos[:, None]
    segment_id = lax.optimization_barrier(jnp.sum(passed.astype(jnp.int32), axis=1)).astype(jnp.int32)
    seq_start = lax.optimization_barrier(jnp.sum(jnp.where(passed, lengths[None, :], 0), axis=1)).astype(jnp.int32)
    return (packed_pos, segment_id, (packed_pos - seq_start).astype(jnp.int32))

def rotary_tables(position, rotary_dims):
    pair_index = jnp.arange(rotary_dims // 2, dtype=jnp.float32)
    inverse = jnp.power(10000.0, -2.0 * pair_index / rotary_dims)
    angles = position.astype(jnp.float32)[:, None] * inverse[None, :]
    return (jnp.cos(angles), jnp.sin(angles))

def rotate(values, cosine_table, sine_table, rotary_dims):
    half_dim = rotary_dims // 2
    first_half = values[..., :half_dim]
    second_half = values[..., half_dim:rotary_dims]
    remainder = values[..., rotary_dims:]
    cosine = cosine_table[:, None, :]
    sine_part = sine_table[:, None, :]
    return jnp.concatenate([first_half * cosine - second_half * sine_part, second_half * cosine + first_half * sine_part, remainder], axis=-1)

def unrotate(values, cosine_table, sine_table, rotary_dims):
    half_dim = rotary_dims // 2
    first_half = values[..., :half_dim]
    second_half = values[..., half_dim:rotary_dims]
    remainder = values[..., rotary_dims:]
    cosine = cosine_table[:, None, :]
    sine_part = sine_table[:, None, :]
    return jnp.concatenate([first_half * cosine + second_half * sine_part, second_half * cosine - first_half * sine_part, remainder], axis=-1)

def normalize(values, norm_gain, norm_bias):
    average = lax.optimization_barrier(jnp.mean(values, axis=-1, keepdims=True))
    centered = values - average
    inv_std = lax.rsqrt(lax.optimization_barrier(jnp.mean(centered * centered, axis=-1, keepdims=True)) + EPSILON)
    scaled = centered * inv_std
    return (scaled * norm_gain + norm_bias, scaled, inv_std)

def norm_backward(grad_normed, scaled, inv_std, norm_gain):
    grad_scaled = grad_normed * norm_gain
    grad_values = inv_std * (grad_scaled - lax.optimization_barrier(jnp.mean(grad_scaled, axis=-1, keepdims=True)) - scaled * lax.optimization_barrier(jnp.mean(grad_scaled * scaled, axis=-1, keepdims=True)))
    return (grad_values, lax.optimization_barrier(jnp.sum(grad_normed * scaled, axis=0)), lax.optimization_barrier(jnp.sum(grad_normed, axis=0)))

def gelu_slope(values):
    return 0.5 * (1.0 + lax.erf(values * 0.7071067811865476)) + values * jnp.exp(-0.5 * values * values) * 0.3989422804014327

def bias_keep(width):
    feature = jnp.arange(width, dtype=jnp.int32) % HD
    part_index = jnp.arange(3, dtype=jnp.int32)[:, None]
    return jnp.where((part_index == 1) & (feature[None, :] >= ROT), 0.0, 1.0).astype(jnp.float32)

def attention_forward(queries, keys_all, vals_all, allowed):
    scale_factor = queries.shape[2] ** (-0.5)

    def one_head(inputs):
        head_query, head_keys, head_vals = inputs
        scores = jnp.dot(head_query, head_keys.T, preferred_element_type=jnp.float32) * scale_factor
        scores = jnp.where(allowed, scores, MASKED)
        row_peak = lax.optimization_barrier(jnp.max(scores, axis=1, keepdims=True))
        exp_scores = jnp.exp(scores - row_peak)
        row_total = lax.optimization_barrier(jnp.sum(exp_scores, axis=1, keepdims=True))
        attn_probs = exp_scores / row_total
        log_total = row_peak[:, 0] + jnp.log(row_total[:, 0])
        attended = jnp.dot(attn_probs.astype(jnp.bfloat16), head_vals, preferred_element_type=jnp.float32)
        return (attended, log_total)
    return lax.map(one_head, (jnp.swapaxes(queries, 0, 1), jnp.swapaxes(keys_all, 0, 1), jnp.swapaxes(vals_all, 0, 1)))

def attention_backward(queries, keys_all, vals_all, log_total, attn_out, grad_attn, allowed):
    scale_factor = queries.shape[2] ** (-0.5)
    total_rows, head_count, head_dim = queries.shape
    out_heads = attn_out.reshape(total_rows, head_count, head_dim)
    grad_heads = grad_attn.reshape(total_rows, head_count, head_dim)
    row_delta = lax.optimization_barrier(jnp.sum(grad_heads.astype(jnp.float32) * out_heads.astype(jnp.float32), axis=2))

    def one_head(inputs):
        head_query, head_keys, head_vals, head_total, head_grad, head_delta = inputs
        scores = jnp.dot(head_query, head_keys.T, preferred_element_type=jnp.float32) * scale_factor
        scores = jnp.where(allowed, scores, MASKED)
        attn_probs = jnp.exp(scores - head_total[:, None])
        probs_rounded = attn_probs.astype(jnp.bfloat16)
        grad_probs = jnp.dot(head_grad, head_vals.T, preferred_element_type=jnp.float32)
        grad_scores = (attn_probs * (grad_probs - head_delta[:, None])).astype(jnp.bfloat16)
        grad_query = jnp.dot(grad_scores, head_keys, preferred_element_type=jnp.float32) * scale_factor
        grad_keys = jnp.dot(grad_scores.T, head_query, preferred_element_type=jnp.float32) * scale_factor
        grad_vals = jnp.dot(probs_rounded.T, head_grad, preferred_element_type=jnp.float32)
        return (grad_query, grad_keys, grad_vals)
    results = lax.map(one_head, (jnp.swapaxes(queries, 0, 1), jnp.swapaxes(keys_all, 0, 1), jnp.swapaxes(vals_all, 0, 1), log_total, jnp.swapaxes(grad_heads, 0, 1), row_delta.T))
    return tuple((jnp.swapaxes(result_item, 0, 1) for result_item in results))

def layer_forward(hidden, params, position, allowed):
    norm1_gain, norm1_bias, norm2_gain, norm2_bias, qkv_w, qkv_b, dense_w, dense_b, up_w, up_b, down_w, down_b = params
    total_rows = hidden.shape[0]
    hidden_wide = hidden.astype(jnp.float32)
    normed_one, scaled_one, inv_std_one = normalize(hidden_wide, norm1_gain.astype(jnp.float32), norm1_bias.astype(jnp.float32))
    attn_input = normed_one.astype(jnp.bfloat16)
    normed_two = scaled_one * norm2_gain.astype(jnp.float32) + norm2_bias.astype(jnp.float32)
    mlp_input = normed_two.astype(jnp.bfloat16)
    projected = [jnp.dot(attn_input, qkv_w[part_index], preferred_element_type=jnp.float32) + qkv_b[part_index].astype(jnp.float32) for part_index in range(3)]
    cosine_table, sine_table = rotary_tables(position, ROT)
    queries = rotate(projected[0].reshape(total_rows, H, HD), cosine_table, sine_table, ROT).astype(jnp.bfloat16)
    keys_all = rotate(projected[1].reshape(total_rows, H, HD), cosine_table, sine_table, ROT).astype(jnp.bfloat16)
    vals_all = projected[2].reshape(total_rows, H, HD).astype(jnp.bfloat16)
    attended, log_total = attention_forward(queries, keys_all, vals_all, allowed)
    attn_out = jnp.swapaxes(attended, 0, 1).reshape(total_rows, H * HD).astype(jnp.bfloat16)
    up_linear = jnp.dot(mlp_input, up_w, preferred_element_type=jnp.float32) + up_b.astype(jnp.float32)
    act_rounded = jax.nn.gelu(up_linear, approximate=False).astype(jnp.bfloat16)
    total = hidden_wide + jnp.dot(attn_out, dense_w, preferred_element_type=jnp.float32) + jnp.dot(act_rounded, down_w, preferred_element_type=jnp.float32) + dense_b.astype(jnp.float32) + down_b.astype(jnp.float32)
    internals = (attn_input, mlp_input, scaled_one, inv_std_one, queries, keys_all, vals_all, log_total, attn_out, up_linear, act_rounded)
    return (total.astype(jnp.bfloat16), internals)

def layer_backward(params, internals, cotangent, position, allowed):
    norm1_gain, norm1_bias, norm2_gain, norm2_bias, qkv_w, qkv_b, dense_w, dense_b, up_w, up_b, down_w, down_b = params
    attn_input, mlp_input, scaled_one, inv_std_one, queries, keys_all, vals_all, log_total, attn_out, up_linear, act_rounded = internals
    total_rows = cotangent.shape[0]
    cot_wide = cotangent.astype(jnp.float32)
    grad_down_w = jnp.dot(act_rounded.T, cotangent, preferred_element_type=jnp.float32)
    grad_act = jnp.dot(cotangent, down_w.T, preferred_element_type=jnp.float32)
    grad_up = grad_act * gelu_slope(up_linear)
    grad_up_bf = grad_up.astype(jnp.bfloat16)
    grad_up_w = jnp.dot(mlp_input.T, grad_up_bf, preferred_element_type=jnp.float32)
    grad_mlp = jnp.dot(grad_up_bf, up_w.T, preferred_element_type=jnp.float32)
    grad_dense_w = jnp.dot(attn_out.T, cotangent, preferred_element_type=jnp.float32)
    grad_attn = jnp.dot(cotangent, dense_w.T, preferred_element_type=jnp.float32).astype(jnp.bfloat16)
    grad_query, grad_keys, grad_vals = attention_backward(queries, keys_all, vals_all, log_total, attn_out, grad_attn, allowed)
    cosine_table, sine_table = rotary_tables(position, ROT)
    grad_query = unrotate(grad_query, cosine_table, sine_table, ROT).reshape(total_rows, H * HD)
    grad_keys = unrotate(grad_keys, cosine_table, sine_table, ROT).reshape(total_rows, H * HD)
    grad_proj = jnp.stack([grad_query, grad_keys, grad_vals.reshape(total_rows, H * HD)])
    grad_proj_bf = grad_proj.astype(jnp.bfloat16)
    grad_qkv_w = jnp.stack([jnp.dot(attn_input.T, grad_proj_bf[part_index], preferred_element_type=jnp.float32) for part_index in range(3)])
    grad_attn_in = jnp.dot(grad_proj_bf[0], qkv_w[0].T, preferred_element_type=jnp.float32)
    grad_attn_in = grad_attn_in + jnp.dot(grad_proj_bf[1], qkv_w[1].T, preferred_element_type=jnp.float32)
    grad_attn_in = grad_attn_in + jnp.dot(grad_proj_bf[2], qkv_w[2].T, preferred_element_type=jnp.float32)
    grad_one, gain_one, shift_one = norm_backward(grad_attn_in, scaled_one, inv_std_one, norm1_gain.astype(jnp.float32))
    grad_two, gain_two, shift_two = norm_backward(grad_mlp, scaled_one, inv_std_one, norm2_gain.astype(jnp.float32))
    grad_hidden = (cot_wide + grad_one + grad_two).astype(jnp.bfloat16)
    bias_sum = lax.optimization_barrier(jnp.sum(cot_wide, axis=0))
    qkv_bias_sum = lax.optimization_barrier(jnp.sum(grad_proj, axis=1)) * bias_keep(H * HD)
    grads_out = (gain_one, shift_one, gain_two, shift_two, grad_qkv_w, qkv_bias_sum, grad_dense_w, bias_sum, grad_up_w, lax.optimization_barrier(jnp.sum(grad_up, axis=0)), grad_down_w, bias_sum)
    return (grad_hidden, grads_out)

def reference(layer_input, out_cotangent, seq_lengths, block_order, ln1_gain, ln1_bias, ln2_gain, ln2_bias, qkv_weight, qkv_bias, dense_weight, dense_bias, up_weight, up_bias, down_weight, down_bias):
    params_all = (ln1_gain, ln1_bias, ln2_gain, ln2_bias, qkv_weight, qkv_bias, dense_weight, dense_bias, up_weight, up_bias, down_weight, down_bias)
    first_params = tuple((leaf_array[0] for leaf_array in params_all))
    second_params = tuple((leaf_array[1] for leaf_array in params_all))

    def micro_step(grad_sum, inputs):
        hidden_in, cotangent, lengths, block_perm = inputs
        packed_pos, segment_id, position = packed_layout(lengths, block_perm, BLK)
        allowed = (segment_id[:, None] == segment_id[None, :]) & (packed_pos[None, :] <= packed_pos[:, None])
        middle, first_state = layer_forward(hidden_in, first_params, position, allowed)
        final, second_state = layer_forward(middle, second_params, position, allowed)
        grad_middle, second_grads = layer_backward(second_params, second_state, cotangent, position, allowed)
        grad_input, first_grads = layer_backward(first_params, first_state, grad_middle, position, allowed)
        stacked = tuple((jnp.stack([first_grads[slot], second_grads[slot]]) for slot in range(12)))
        grad_sum = tuple((grad_sum[slot] + stacked[slot] for slot in range(12)))
        return (grad_sum, (jnp.stack([middle, final]), jnp.stack([grad_input, grad_middle])))
    zeros_init = tuple((jnp.zeros(leaf_array.shape, jnp.float32) for leaf_array in params_all))
    grad_sum, (outs_stacked, grads_stacked) = lax.scan(micro_step, zeros_init, (layer_input, out_cotangent, seq_lengths, block_order))
    layer_out = jnp.swapaxes(outs_stacked, 0, 1)
    input_grad = jnp.swapaxes(grads_stacked, 0, 1)
    return (layer_out, input_grad, grad_sum[0], grad_sum[1], grad_sum[2], grad_sum[3], grad_sum[4], grad_sum[5], grad_sum[6], grad_sum[7], grad_sum[8], grad_sum[9], grad_sum[10], grad_sum[11])
```

```python
import jax
import jax.numpy as jnp
from jax import lax
from jax.sharding import PartitionSpec as P

HD = 64
ROT = 16


EPSILON = 1e-05
MASKED = -1e30


def shifted(x, axis, by):
    count = lax.axis_size(axis)
    pairs = [(i, i + by) for i in range(count) if 0 <= i + by < count]
    return lax.ppermute(x, axis, pairs)


def packed_layout(lengths, block_perm, block_rows):
    total_rows = block_perm.shape[0] * block_rows
    row_index = jnp.arange(total_rows, dtype=jnp.int32)
    chosen = (row_index // block_rows)[:, None] == jnp.arange(block_perm.shape[0], dtype=jnp.int32)[
        None, :
    ]
    packed_pos = (
        jnp.sum(jnp.where(chosen, block_perm[None, :], 0), axis=1) * block_rows
        + row_index % block_rows
    )
    seq_ends = jnp.cumsum(lengths)
    passed = seq_ends[None, :] <= packed_pos[:, None]
    segment_id = jnp.sum(passed.astype(jnp.int32), axis=1)
    seq_start = jnp.sum(jnp.where(passed, lengths[None, :], 0), axis=1)
    return (packed_pos, segment_id, packed_pos - seq_start)


def micro_layout(seq_lengths, block_order, micro_index, block_rows, context_index, tok_rows):
    lengths = lax.dynamic_index_in_dim(seq_lengths, micro_index, 0, keepdims=False)
    block_perm = lax.dynamic_index_in_dim(block_order, micro_index, 0, keepdims=False)
    packed_pos, segment_id, position = packed_layout(lengths, block_perm, block_rows)
    local_start = context_index * tok_rows
    my_packed = lax.dynamic_slice_in_dim(packed_pos, local_start, tok_rows)
    my_segment = lax.dynamic_slice_in_dim(segment_id, local_start, tok_rows)
    my_position = lax.dynamic_slice_in_dim(position, local_start, tok_rows)
    allowed = (my_segment[:, None] == segment_id[None, :]) & (
        packed_pos[None, :] <= my_packed[:, None]
    )
    allowed_cols = (segment_id[:, None] == my_segment[None, :]) & (
        my_packed[None, :] <= packed_pos[:, None]
    )
    return (my_position, allowed, allowed_cols)


def rotary_tables(position, rotary_dims):
    pair_index = jnp.arange(rotary_dims // 2, dtype=jnp.float32)
    inverse = jnp.power(10000.0, -2.0 * pair_index / rotary_dims)
    angles = position.astype(jnp.float32)[:, None] * inverse[None, :]
    return (jnp.cos(angles), jnp.sin(angles))


def rotate(values, cosine_table, sine_table, rotary_dims):
    half_dim = rotary_dims // 2
    first_half = values[..., :half_dim]
    second_half = values[..., half_dim:rotary_dims]
    remainder = values[..., rotary_dims:]
    cosine = cosine_table[:, None, :]
    sine_part = sine_table[:, None, :]
    return jnp.concatenate(
        [
            first_half * cosine - second_half * sine_part,
            second_half * cosine + first_half * sine_part,
            remainder,
        ],
        axis=-1,
    )


def unrotate(values, cosine_table, sine_table, rotary_dims):
    half_dim = rotary_dims // 2
    first_half = values[..., :half_dim]
    second_half = values[..., half_dim:rotary_dims]
    remainder = values[..., rotary_dims:]
    cosine = cosine_table[:, None, :]
    sine_part = sine_table[:, None, :]
    return jnp.concatenate(
        [
            first_half * cosine + second_half * sine_part,
            second_half * cosine - first_half * sine_part,
            remainder,
        ],
        axis=-1,
    )


def normalize(values, norm_gain, norm_bias):
    average = jnp.mean(values, axis=-1, keepdims=True)
    centered = values - average
    inv_std = lax.rsqrt(jnp.mean(centered * centered, axis=-1, keepdims=True) + EPSILON)
    scaled = centered * inv_std
    return (scaled * norm_gain + norm_bias, scaled, inv_std)


def norm_backward(grad_normed, scaled, inv_std, norm_gain):
    grad_scaled = grad_normed * norm_gain
    grad_values = inv_std * (
        grad_scaled
        - jnp.mean(grad_scaled, axis=-1, keepdims=True)
        - scaled * jnp.mean(grad_scaled * scaled, axis=-1, keepdims=True)
    )
    return (grad_values, jnp.sum(grad_normed * scaled, axis=0), jnp.sum(grad_normed, axis=0))


def gelu_slope(values):
    return (
        0.5 * (1.0 + lax.erf(values * 0.7071067811865476))
        + values * jnp.exp(-0.5 * values * values) * 0.3989422804014327
    )


def bias_keep(width):
    feature = jnp.arange(width, dtype=jnp.int32) % HD
    part_index = jnp.arange(3, dtype=jnp.int32)[:, None]
    return jnp.where((part_index == 1) & (feature[None, :] >= ROT), 0.0, 1.0).astype(jnp.float32)


def gather_weights(shards):
    return (
        lax.all_gather(shards[0], "context", axis=0, tiled=True),
        lax.all_gather(shards[1], "context", axis=0, tiled=True),
        lax.all_gather(shards[2], "context", axis=0, tiled=True),
        lax.all_gather(shards[3], "context", axis=0, tiled=True),
        lax.all_gather(shards[4], "context", axis=1, tiled=True),
        lax.all_gather(shards[5], "context", axis=1, tiled=True),
        lax.all_gather(shards[6], "context", axis=1, tiled=True),
        lax.all_gather(shards[7], "context", axis=0, tiled=True),
        lax.all_gather(shards[8], "context", axis=0, tiled=True),
        lax.all_gather(shards[9], "context", axis=0, tiled=True),
        lax.all_gather(shards[10], "context", axis=1, tiled=True),
        lax.all_gather(shards[11], "context", axis=0, tiled=True),
    )


def split_pairs(pair_all, local_heads):
    total_rows = pair_all.shape[0]
    local_width = pair_all.shape[1] // 2
    keys_all = pair_all[:, :local_width].reshape(total_rows, local_heads, HD)
    vals_all = pair_all[:, local_width:].reshape(total_rows, local_heads, HD)
    return (keys_all, vals_all)


def attention_forward(queries, pair_all, allowed):
    keys_all, vals_all = split_pairs(pair_all, queries.shape[1])
    scale_factor = HD ** (-0.5)
    scores = (
        jnp.einsum("qhd,khd->hqk", queries, keys_all, preferred_element_type=jnp.float32)
        * scale_factor
    )
    scores = jnp.where(allowed[None], scores, MASKED)
    row_peak = jnp.max(scores, axis=2, keepdims=True)
    exp_scores = jnp.exp(scores - row_peak)
    row_total = jnp.sum(exp_scores, axis=2, keepdims=True)
    attn_probs = exp_scores / row_total
    log_total = row_peak[..., 0] + jnp.log(row_total[..., 0])
    attended = jnp.einsum(
        "hqk,khd->qhd",
        attn_probs.astype(jnp.bfloat16),
        vals_all,
        preferred_element_type=jnp.float32,
    )
    return (attended, log_total)


def attention_backward(queries, pair_all, log_total, attn_out, grad_attn, allowed):
    tok_rows, local_heads = (queries.shape[0], queries.shape[1])
    total_rows = pair_all.shape[0]
    local_width = local_heads * HD
    keys_all, vals_all = split_pairs(pair_all, local_heads)
    scale_factor = HD ** (-0.5)
    scores = (
        jnp.einsum("qhd,khd->hqk", queries, keys_all, preferred_element_type=jnp.float32)
        * scale_factor
    )
    scores = jnp.where(allowed[None], scores, MASKED)
    attn_probs = jnp.exp(scores - log_total[:, :, None])
    grad_heads = grad_attn.reshape(tok_rows, local_heads, HD)
    row_delta = jnp.sum(
        grad_heads.astype(jnp.float32)
        * attn_out.reshape(tok_rows, local_heads, HD).astype(jnp.float32),
        axis=2,
    )
    grad_probs = jnp.einsum(
        "qhd,khd->hqk", grad_heads, vals_all, preferred_element_type=jnp.float32
    )
    grad_scores = (attn_probs * (grad_probs - jnp.transpose(row_delta)[:, :, None])).astype(
        jnp.bfloat16
    )
    grad_query = (
        jnp.einsum("hqk,khd->qhd", grad_scores, keys_all, preferred_element_type=jnp.float32)
        * scale_factor
    )
    probs_rounded = attn_probs.astype(jnp.bfloat16)
    grad_keys = (
        jnp.einsum("hqk,qhd->khd", grad_scores, queries, preferred_element_type=jnp.float32)
        * scale_factor
    )
    grad_vals = jnp.einsum(
        "hqk,qhd->khd", probs_rounded, grad_heads, preferred_element_type=jnp.float32
    )
    key_terms = jnp.concatenate(
        [grad_keys.reshape(total_rows, local_width), grad_vals.reshape(total_rows, local_width)],
        axis=1,
    )
    own_rows = lax.psum_scatter(key_terms, "context", scatter_dimension=0, tiled=True)
    return (
        grad_query,
        own_rows[:, :local_width].reshape(tok_rows, local_heads, HD),
        own_rows[:, local_width:],
    )


def layer_forward(hidden, weights, my_position, allowed):
    (
        norm1_gain,
        norm1_bias,
        norm2_gain,
        norm2_bias,
        qkv_w,
        qkv_b,
        dense_w,
        dense_b,
        up_w,
        up_b,
        down_w,
        down_b,
    ) = weights
    tok_rows = hidden.shape[0]
    local_width = qkv_w.shape[2]
    local_heads = local_width // HD
    hidden_wide = hidden.astype(jnp.float32)
    normed_one, scaled_one, inv_std_one = normalize(
        hidden_wide, norm1_gain.astype(jnp.float32), norm1_bias.astype(jnp.float32)
    )
    attn_input = normed_one.astype(jnp.bfloat16)
    mlp_input = (
        scaled_one * norm2_gain.astype(jnp.float32) + norm2_bias.astype(jnp.float32)
    ).astype(jnp.bfloat16)
    projected = (
        jnp.einsum("td,cde->cte", attn_input, qkv_w, preferred_element_type=jnp.float32)
        + qkv_b.astype(jnp.float32)[:, None, :]
    )
    cosine_table, sine_table = rotary_tables(my_position, ROT)
    queries = rotate(
        projected[0].reshape(tok_rows, local_heads, HD), cosine_table, sine_table, ROT
    ).astype(jnp.bfloat16)
    key_rows = rotate(
        projected[1].reshape(tok_rows, local_heads, HD), cosine_table, sine_table, ROT
    ).astype(jnp.bfloat16)
    value_rows = projected[2].astype(jnp.bfloat16)
    pair_local = jnp.concatenate([key_rows.reshape(tok_rows, local_width), value_rows], axis=1)
    pair_all = lax.all_gather(pair_local, "context", axis=0, tiled=True)
    attended, log_total = attention_forward(queries, pair_all, allowed)
    attn_out = attended.reshape(tok_rows, local_width).astype(jnp.bfloat16)
    up_linear = jnp.dot(mlp_input, up_w, preferred_element_type=jnp.float32) + up_b.astype(
        jnp.float32
    )
    act_rounded = jax.nn.gelu(up_linear, approximate=False).astype(jnp.bfloat16)
    branch_terms = jnp.dot(attn_out, dense_w, preferred_element_type=jnp.float32) + jnp.dot(
        act_rounded, down_w, preferred_element_type=jnp.float32
    )
    summed = lax.psum(branch_terms, "tensor")
    output = (
        hidden_wide + summed + dense_b.astype(jnp.float32) + down_b.astype(jnp.float32)
    ).astype(jnp.bfloat16)
    kept_state = (hidden, queries, pair_local, log_total, attn_out, up_linear, pair_all)
    return (output, kept_state)


def layer_backward(kept_state, cotangent, weights, my_position, allowed):
    (
        norm1_gain,
        norm1_bias,
        norm2_gain,
        norm2_bias,
        qkv_w,
        qkv_b,
        dense_w,
        dense_b,
        up_w,
        up_b,
        down_w,
        down_b,
    ) = weights
    hidden, queries, pair_local, log_total, attn_out, up_linear = (
        kept_state[0],
        kept_state[1],
        kept_state[2],
        kept_state[3],
        kept_state[4],
        kept_state[5],
    )
    pair_all = kept_state[6]
    tok_rows = hidden.shape[0]
    local_width = qkv_w.shape[2]
    hidden_wide = hidden.astype(jnp.float32)
    normed_one, scaled_one, inv_std_one = normalize(
        hidden_wide, norm1_gain.astype(jnp.float32), norm1_bias.astype(jnp.float32)
    )
    attn_input = normed_one.astype(jnp.bfloat16)
    mlp_input = (
        scaled_one * norm2_gain.astype(jnp.float32) + norm2_bias.astype(jnp.float32)
    ).astype(jnp.bfloat16)
    cot_wide = cotangent.astype(jnp.float32)
    act_rounded = jax.nn.gelu(up_linear, approximate=False).astype(jnp.bfloat16)
    grad_down_w = jnp.einsum(
        "tf,td->fd", act_rounded, cotangent, preferred_element_type=jnp.float32
    )
    grad_act = jnp.einsum("td,fd->tf", cotangent, down_w, preferred_element_type=jnp.float32)
    grad_up = grad_act * gelu_slope(up_linear)
    grad_up_bf = grad_up.astype(jnp.bfloat16)
    grad_up_w = jnp.einsum("td,tf->df", mlp_input, grad_up_bf, preferred_element_type=jnp.float32)
    grad_mlp = jnp.einsum("tf,df->td", grad_up_bf, up_w, preferred_element_type=jnp.float32)
    grad_dense_w = jnp.einsum("te,td->ed", attn_out, cotangent, preferred_element_type=jnp.float32)
    grad_attn = jnp.einsum(
        "td,ed->te", cotangent, dense_w, preferred_element_type=jnp.float32
    ).astype(jnp.bfloat16)
    grad_query, grad_keys, grad_vals = attention_backward(
        queries, pair_all, log_total, attn_out, grad_attn, allowed
    )
    cosine_table, sine_table = rotary_tables(my_position, ROT)
    grad_query = unrotate(grad_query, cosine_table, sine_table, ROT).reshape(tok_rows, local_width)
    grad_keys = unrotate(grad_keys, cosine_table, sine_table, ROT).reshape(tok_rows, local_width)
    grad_proj = jnp.stack([grad_query, grad_keys, grad_vals])
    grad_proj_bf = grad_proj.astype(jnp.bfloat16)
    grad_qkv_w = jnp.einsum(
        "td,cte->cde", attn_input, grad_proj_bf, preferred_element_type=jnp.float32
    )
    grad_attn_in = jnp.einsum(
        "cte,cde->td", grad_proj_bf, qkv_w, preferred_element_type=jnp.float32
    )
    grad_attn_in, grad_mlp = lax.psum((grad_attn_in, grad_mlp), "tensor")
    grad_one, gain_one, shift_one = norm_backward(
        grad_attn_in, scaled_one, inv_std_one, norm1_gain.astype(jnp.float32)
    )
    grad_two, gain_two, shift_two = norm_backward(
        grad_mlp, scaled_one, inv_std_one, norm2_gain.astype(jnp.float32)
    )
    grad_hidden = (cot_wide + grad_one + grad_two).astype(jnp.bfloat16)
    bias_sum = jnp.sum(cot_wide, axis=0)
    qkv_bias_sum = jnp.sum(grad_proj, axis=1) * bias_keep(local_width)
    layer_grads = (
        gain_one,
        shift_one,
        gain_two,
        shift_two,
        grad_qkv_w,
        qkv_bias_sum,
        grad_dense_w,
        bias_sum,
        grad_up_w,
        jnp.sum(grad_up, axis=0),
        grad_down_w,
        bias_sum,
    )
    return (grad_hidden, layer_grads)


def body(
    layer_input,
    out_cotangent,
    seq_lengths,
    block_order,
    ln1_gain,
    ln1_bias,
    ln2_gain,
    ln2_bias,
    qkv_weight,
    qkv_bias,
    dense_weight,
    dense_bias,
    up_weight,
    up_bias,
    down_weight,
    down_bias,
):
    section_index = lax.axis_index("section")
    context_index = lax.axis_index("context")
    micro_count = layer_input.shape[0]
    tok_rows = layer_input.shape[1]
    block_rows = tok_rows // 2
    shards = (
        ln1_gain[0],
        ln1_bias[0],
        ln2_gain[0],
        ln2_bias[0],
        qkv_weight[0],
        qkv_bias[0],
        dense_weight[0],
        dense_bias[0],
        up_weight[0],
        up_bias[0],
        down_weight[0],
        down_bias[0],
    )
    forward_outs = []
    state_list = []
    incoming = jnp.zeros_like(layer_input[0])
    for tick_index in range(micro_count + 1):
        micro_index = jnp.clip(tick_index - section_index, 0, micro_count - 1)
        hidden = jnp.where(
            section_index == 0, layer_input[min(tick_index, micro_count - 1)], incoming
        )
        weights = gather_weights(shards)
        my_position, allowed, allowed_cols = micro_layout(
            seq_lengths, block_order, micro_index, block_rows, context_index, tok_rows
        )
        output, kept_state = layer_forward(hidden, weights, my_position, allowed)
        forward_outs.append(output)
        state_list.append(kept_state)
        if tick_index < micro_count:
            incoming = shifted(output, "section", 1)
    stacked_outs = jnp.stack(forward_outs)
    layer_out = jnp.where(section_index == 0, stacked_outs[:micro_count], stacked_outs[1:])
    state_stack = jax.tree.map(lambda *leaves: jnp.stack(leaves), *state_list)
    grad_totals = None
    backward_outs = []
    incoming_grad = jnp.zeros_like(out_cotangent[0])
    for tick_index in range(micro_count + 1):
        micro_raw = tick_index - 1 + section_index
        is_valid = (micro_raw >= 0) & (micro_raw < micro_count)
        micro_index = jnp.clip(micro_raw, 0, micro_count - 1)
        state_index = jnp.clip(micro_raw + section_index, 0, micro_count)
        kept_state = jax.tree.map(
            lambda leaf_array: lax.dynamic_index_in_dim(leaf_array, state_index, 0, keepdims=False),
            state_stack,
        )
        cotangent = jnp.where(
            section_index == 1, out_cotangent[min(tick_index, micro_count - 1)], incoming_grad
        )
        weights = gather_weights(shards)
        my_position, allowed, allowed_cols = micro_layout(
            seq_lengths, block_order, micro_index, block_rows, context_index, tok_rows
        )
        grad_hidden, layer_grads = layer_backward(
            kept_state, cotangent, weights, my_position, allowed
        )
        layer_grads = jax.tree.map(
            lambda leaf_array: jnp.where(is_valid, leaf_array, 0.0), layer_grads
        )
        grad_totals = (
            layer_grads if grad_totals is None else jax.tree.map(jnp.add, grad_totals, layer_grads)
        )
        backward_outs.append(grad_hidden)
        if tick_index < micro_count:
            incoming_grad = shifted(grad_hidden, "section", -1)
    stacked_grads = jnp.stack(backward_outs)
    input_grad = jnp.where(section_index == 1, stacked_grads[:micro_count], stacked_grads[1:])
    owned_grads = (
        lax.psum_scatter(
            grad_totals[0].astype(jnp.bfloat16), "context", scatter_dimension=0, tiled=True
        ).astype(jnp.float32),
        lax.psum_scatter(
            grad_totals[1].astype(jnp.bfloat16), "context", scatter_dimension=0, tiled=True
        ).astype(jnp.float32),
        lax.psum_scatter(
            grad_totals[2].astype(jnp.bfloat16), "context", scatter_dimension=0, tiled=True
        ).astype(jnp.float32),
        lax.psum_scatter(
            grad_totals[3].astype(jnp.bfloat16), "context", scatter_dimension=0, tiled=True
        ).astype(jnp.float32),
        lax.psum_scatter(
            grad_totals[4].astype(jnp.bfloat16), "context", scatter_dimension=1, tiled=True
        ).astype(jnp.float32),
        lax.psum_scatter(
            grad_totals[5].astype(jnp.bfloat16), "context", scatter_dimension=1, tiled=True
        ).astype(jnp.float32),
        lax.psum_scatter(
            grad_totals[6].astype(jnp.bfloat16), "context", scatter_dimension=1, tiled=True
        ).astype(jnp.float32),
        lax.psum_scatter(
            grad_totals[7].astype(jnp.bfloat16), "context", scatter_dimension=0, tiled=True
        ).astype(jnp.float32),
        lax.psum_scatter(
            grad_totals[8].astype(jnp.bfloat16), "context", scatter_dimension=0, tiled=True
        ).astype(jnp.float32),
        lax.psum_scatter(
            grad_totals[9].astype(jnp.bfloat16), "context", scatter_dimension=0, tiled=True
        ).astype(jnp.float32),
        lax.psum_scatter(
            grad_totals[10].astype(jnp.bfloat16), "context", scatter_dimension=1, tiled=True
        ).astype(jnp.float32),
        lax.psum_scatter(
            grad_totals[11].astype(jnp.bfloat16), "context", scatter_dimension=0, tiled=True
        ).astype(jnp.float32),
    )
    return (
        layer_out[None],
        input_grad[None],
        owned_grads[0][None],
        owned_grads[1][None],
        owned_grads[2][None],
        owned_grads[3][None],
        owned_grads[4][None],
        owned_grads[5][None],
        owned_grads[6][None],
        owned_grads[7][None],
        owned_grads[8][None],
        owned_grads[9][None],
        owned_grads[10][None],
        owned_grads[11][None],
    )


def wide_attention(queries, keys, vals, allowed):
    scores = jnp.einsum("qhd,khd->hqk", queries, keys, preferred_element_type=jnp.float32)
    scores = jnp.where(allowed[None], scores * HD ** (-0.5), MASKED)
    row_peak = jnp.max(scores, axis=2, keepdims=True)
    exp_scores = jnp.exp(scores - row_peak)
    probs = exp_scores / jnp.sum(exp_scores, axis=2, keepdims=True)
    attended = jnp.einsum(
        "hqk,khd->qhd", probs.astype(jnp.bfloat16), vals, preferred_element_type=jnp.float32
    )
    return (attended, probs)


def sum_parts(parts):
    return lax.psum(parts.astype(jnp.bfloat16), ("tensor", "context")).astype(jnp.float32)


def wide_forward(hidden, weights, tables, allowed):
    gain1, bias1, gain2, bias2, dense_b, down_b, qkv_w, qkv_b, dense_w, up_w, up_b, down_w = weights
    rows = hidden.shape[0]
    width = qkv_w.shape[2]
    heads = width // HD
    hidden_wide = hidden.astype(jnp.float32)
    normed, scaled, inv_std = normalize(hidden_wide, gain1, bias1)
    attn_input = normed.astype(jnp.bfloat16)
    mlp_input = (scaled * gain2 + bias2).astype(jnp.bfloat16)
    projected = (
        jnp.einsum("td,cde->cte", attn_input, qkv_w, preferred_element_type=jnp.float32)
        + qkv_b[:, None, :]
    )
    queries = rotate(projected[0].reshape(rows, heads, HD), *tables, ROT).astype(jnp.bfloat16)
    keys = rotate(projected[1].reshape(rows, heads, HD), *tables, ROT).astype(jnp.bfloat16)
    vals = projected[2].astype(jnp.bfloat16).reshape(rows, heads, HD)
    attended, probs = wide_attention(queries, keys, vals, allowed)
    attn_out = attended.reshape(rows, width).astype(jnp.bfloat16)
    up_linear = jnp.dot(mlp_input, up_w, preferred_element_type=jnp.float32) + up_b
    act = jax.nn.gelu(up_linear, approximate=False).astype(jnp.bfloat16)
    parts = jnp.dot(attn_out, dense_w, preferred_element_type=jnp.float32) + jnp.dot(
        act, down_w, preferred_element_type=jnp.float32
    )
    output = (hidden_wide + sum_parts(parts) + (dense_b + down_b)).astype(jnp.bfloat16)
    state = (attn_input, mlp_input, scaled, inv_std, queries, keys, vals, probs, attn_out, up_linear, act)
    return (output, state)


def wide_backward(state, cotangent, weights, tables):
    gain1, bias1, gain2, bias2, dense_b, down_b, qkv_w, qkv_b, dense_w, up_w, up_b, down_w = weights
    attn_input, mlp_input, scaled, inv_std, queries, keys, vals, probs, attn_out, up_linear, act = state
    rows = cotangent.shape[0]
    width = qkv_w.shape[2]
    heads = width // HD
    f32 = jnp.float32
    cot_wide = cotangent.astype(f32)
    grad_act = jnp.einsum("td,fd->tf", cotangent, down_w, preferred_element_type=f32)
    grad_up = grad_act * gelu_slope(up_linear)
    grad_up_bf = grad_up.astype(jnp.bfloat16)
    grad_attn = jnp.einsum("td,ed->te", cotangent, dense_w, preferred_element_type=f32).astype(
        jnp.bfloat16
    )
    grad_heads = grad_attn.reshape(rows, heads, HD)
    delta = jnp.sum(
        grad_heads.astype(f32) * attn_out.reshape(rows, heads, HD).astype(f32), axis=2
    )
    grad_probs = jnp.einsum("qhd,khd->hqk", grad_heads, vals, preferred_element_type=f32)
    grad_scores = (probs * (grad_probs - jnp.transpose(delta)[:, :, None])).astype(jnp.bfloat16)
    scale = HD ** (-0.5)
    grad_q = jnp.einsum("hqk,khd->qhd", grad_scores, keys, preferred_element_type=f32) * scale
    grad_k = jnp.einsum("hqk,qhd->khd", grad_scores, queries, preferred_element_type=f32) * scale
    grad_v = jnp.einsum(
        "hqk,qhd->khd", probs.astype(jnp.bfloat16), grad_heads, preferred_element_type=f32
    )
    grad_proj = jnp.stack(
        [
            unrotate(grad_q, *tables, ROT).reshape(rows, width),
            unrotate(grad_k, *tables, ROT).reshape(rows, width),
            grad_v.reshape(rows, width),
        ]
    )
    grad_proj_bf = grad_proj.astype(jnp.bfloat16)
    grad_a1 = jnp.einsum("cte,cde->td", grad_proj_bf, qkv_w, preferred_element_type=f32)
    grad_a2 = jnp.einsum("tf,df->td", grad_up_bf, up_w, preferred_element_type=f32)
    total = sum_parts(grad_a1 * gain1 + grad_a2 * gain2)
    grad_hidden = (
        cot_wide
        + inv_std
        * (
            total
            - jnp.mean(total, axis=-1, keepdims=True)
            - scaled * jnp.mean(total * scaled, axis=-1, keepdims=True)
        )
    ).astype(jnp.bfloat16)
    shared = jnp.stack(
        [
            jnp.sum(grad_a1 * scaled, axis=0),
            jnp.sum(grad_a1, axis=0),
            jnp.sum(grad_a2 * scaled, axis=0),
            jnp.sum(grad_a2, axis=0),
        ]
    )
    first = (lax.axis_index("tensor") == 0) & (lax.axis_index("context") == 0)
    bias_sum = jnp.where(first, jnp.sum(cot_wide, axis=0), 0.0)
    shared = jnp.concatenate([shared, bias_sum[None]], axis=0)
    own = jnp.concatenate(
        [
            (jnp.sum(grad_proj, axis=1) * bias_keep(width)).reshape(-1),
            jnp.sum(grad_up, axis=0),
        ]
    )
    grad_w = (
        jnp.einsum("td,cte->cde", attn_input, grad_proj_bf, preferred_element_type=f32),
        jnp.einsum("te,td->ed", attn_out, cotangent, preferred_element_type=f32),
        jnp.einsum("td,tf->df", mlp_input, grad_up_bf, preferred_element_type=f32),
        jnp.einsum("tf,td->fd", act, cotangent, preferred_element_type=f32),
    )
    return (grad_hidden, shared, own, grad_w)


def swap_sections(pair):
    section = lax.axis_index("section")
    theirs = lax.dynamic_index_in_dim(pair, 1 - section, 0, keepdims=False)
    mine = lax.dynamic_index_in_dim(pair, section, 0, keepdims=False)
    return (mine, lax.ppermute(theirs, "section", [(0, 1), (1, 0)]))


def wide_body(
    layer_input,
    out_cotangent,
    seq_lengths,
    block_order,
    ln1_gain,
    ln1_bias,
    ln2_gain,
    ln2_bias,
    qkv_weight,
    qkv_bias,
    dense_weight,
    dense_bias,
    up_weight,
    up_bias,
    down_weight,
    down_bias,
):
    f32 = jnp.float32
    bf16 = jnp.bfloat16
    section = lax.axis_index("section")
    context = lax.axis_index("context")
    tok_rows = layer_input.shape[1]
    block_rows = tok_rows * lax.axis_size("context") // block_order.shape[1]
    edges = jnp.stack(
        [
            lax.dynamic_index_in_dim(layer_input, section, 0, keepdims=False),
            lax.dynamic_index_in_dim(out_cotangent, section, 0, keepdims=False),
        ]
    )
    edges = lax.all_gather(edges, "context", axis=1, tiled=True)
    vectors = jnp.concatenate([ln1_gain, ln1_bias, ln2_gain, ln2_bias, dense_bias, down_bias], axis=0)
    vectors = lax.all_gather(
        lax.all_gather(vectors, "context", axis=1, tiled=True), "section", axis=0
    ).astype(f32)
    own_bias = lax.all_gather(
        jnp.concatenate([qkv_bias[0].reshape(-1), up_bias[0]]), "section", axis=0
    ).astype(f32)
    width = qkv_bias.shape[2]
    matrices = (
        lax.all_to_all(qkv_weight[0], "context", 2, 1, tiled=True),
        lax.all_to_all(dense_weight[0], "context", 0, 1, tiled=True),
        lax.all_to_all(up_weight[0], "context", 1, 0, tiled=True),
        lax.all_to_all(down_weight[0], "context", 0, 1, tiled=True),
    )
    matrices = tuple(lax.all_gather(leaf, "section", axis=0) for leaf in matrices)
    weights = [
        (
            *(vectors[layer, i] for i in range(6)),
            matrices[0][layer],
            own_bias[layer, : 3 * width].reshape(3, width),
            matrices[1][layer],
            matrices[2][layer],
            own_bias[layer, 3 * width :],
            matrices[3][layer],
        )
        for layer in range(2)
    ]
    lengths = lax.dynamic_index_in_dim(seq_lengths, section, 0, keepdims=False)
    perm = lax.dynamic_index_in_dim(block_order, section, 0, keepdims=False)
    packed_pos, segment_id, position = packed_layout(lengths, perm, block_rows)
    allowed = (segment_id[:, None] == segment_id[None, :]) & (
        packed_pos[None, :] <= packed_pos[:, None]
    )
    tables = rotary_tables(position, ROT)
    hidden = edges[0]
    states = []
    outs = []
    for layer in range(2):
        hidden, state = wide_forward(hidden, weights[layer], tables, allowed)
        outs.append(hidden)
        states.append(state)
    cotangent = edges[1]
    grads = [None, None]
    cots = [None, None]
    for layer in (1, 0):
        cotangent, shared, own, grad_w = wide_backward(
            states[layer], cotangent, weights[layer], tables
        )
        cots[layer] = cotangent
        grads[layer] = (shared, own, grad_w)
    both = jnp.stack([jnp.stack([outs[layer], cots[layer]]) for layer in range(2)])
    both = lax.dynamic_slice_in_dim(both, context * tok_rows, tok_rows, 2)
    mine, theirs = swap_sections(both)
    low = jnp.where(section == 0, mine, theirs)
    high = jnp.where(section == 0, theirs, mine)
    layer_out = jnp.stack([low[0], high[0]])
    input_grad = jnp.stack([low[1], high[1]])
    shared = jnp.stack([grads[0][0], grads[1][0]])
    shared = lax.psum(shared, ("section", "tensor", "context"))
    shared = lax.dynamic_index_in_dim(shared, section, 0, keepdims=False)
    cols = ln1_gain.shape[1]
    shared = lax.dynamic_slice_in_dim(shared, context * cols, cols, 1)
    mine, theirs = swap_sections(jnp.stack([grads[0][1], grads[1][1]]))
    own = mine + theirs
    summed = []
    for i in range(4):
        pair = jnp.stack([grads[0][2][i], grads[1][2][i]])
        mine = lax.dynamic_index_in_dim(pair, section, 0, keepdims=False)
        theirs = lax.dynamic_index_in_dim(pair, 1 - section, 0, keepdims=False).astype(bf16)
        summed.append(
            (mine + lax.ppermute(theirs, "section", [(0, 1), (1, 0)]).astype(f32)).astype(bf16)
        )
    qkv_g = lax.all_to_all(summed[0], "context", 1, 2, tiled=True).astype(f32)
    dense_g = lax.all_to_all(summed[1], "context", 1, 0, tiled=True).astype(f32)
    up_g = lax.all_to_all(summed[2], "context", 0, 1, tiled=True).astype(f32)
    down_g = lax.all_to_all(summed[3], "context", 1, 0, tiled=True).astype(f32)
    return (
        layer_out[None],
        input_grad[None],
        shared[0][None],
        shared[1][None],
        shared[2][None],
        shared[3][None],
        qkv_g[None],
        own[: 3 * width].reshape(1, 3, width),
        dense_g[None],
        shared[4][None],
        up_g[None],
        own[3 * width :][None],
        down_g[None],
        shared[4][None],
    )


def plan(*args):
    heads = args[10].shape[1] // HD
    units = lax.axis_size("context")
    if heads % units == 0 and args[0].shape[0] == lax.axis_size("section") == 2:
        return wide_body(*args)
    return body(*args)


def solution(mesh):
    return jax.shard_map(
        plan,
        mesh=mesh,
        in_specs=(
            P(None, "context", None),
            P(None, "context", None),
            P(),
            P(),
            P("section", "context"),
            P("section", "context"),
            P("section", "context"),
            P("section", "context"),
            P("section", None, "context", "tensor"),
            P("section", None, ("tensor", "context")),
            P("section", "tensor", "context"),
            P("section", "context"),
            P("section", "context", "tensor"),
            P("section", ("tensor", "context")),
            P("section", "tensor", "context"),
            P("section", "context"),
        ),
        out_specs=(
            P("section", None, "context", None),
            P("section", None, "context", None),
            P("section", "context"),
            P("section", "context"),
            P("section", "context"),
            P("section", "context"),
            P("section", None, "context", "tensor"),
            P("section", None, ("tensor", "context")),
            P("section", "tensor", "context"),
            P("section", "context"),
            P("section", "context", "tensor"),
            P("section", ("tensor", "context")),
            P("section", "tensor", "context"),
            P("section", "context"),
        ),
        check_vma=False,
    )
```

```python
import functools

import jax
import jax.numpy as jnp
from jax import lax
from jax.experimental import pallas as pl
from jax.experimental.pallas import tpu as pltpu
from jax.sharding import PartitionSpec as P

CTX = "context"
TEN = "tensor"
SEC = "section"
HD = 64
ROT = 16


EPSILON = 1e-05
MASKED = -1e30


def shifted(x, axis, by):
    count = lax.axis_size(axis)
    pairs = [(i, i + by) for i in range(count) if 0 <= i + by < count]
    return lax.ppermute(x, axis, pairs)


def packed_layout(lengths, block_perm, block_rows):
    total_rows = block_perm.shape[0] * block_rows
    row_index = jnp.arange(total_rows, dtype=jnp.int32)
    chosen = (row_index // block_rows)[:, None] == jnp.arange(block_perm.shape[0], dtype=jnp.int32)[
        None, :
    ]
    packed_pos = (
        jnp.sum(jnp.where(chosen, block_perm[None, :], 0), axis=1) * block_rows
        + row_index % block_rows
    )
    seq_ends = jnp.cumsum(lengths)
    passed = seq_ends[None, :] <= packed_pos[:, None]
    segment_id = jnp.sum(passed.astype(jnp.int32), axis=1)
    seq_start = jnp.sum(jnp.where(passed, lengths[None, :], 0), axis=1)
    return (packed_pos, segment_id, packed_pos - seq_start)


def micro_layout(seq_lengths, block_order, micro_index, block_rows, context_index, tok_rows):
    lengths = lax.dynamic_index_in_dim(seq_lengths, micro_index, 0, keepdims=False)
    block_perm = lax.dynamic_index_in_dim(block_order, micro_index, 0, keepdims=False)
    packed_pos, segment_id, position = packed_layout(lengths, block_perm, block_rows)
    local_start = context_index * tok_rows
    my_packed = lax.dynamic_slice_in_dim(packed_pos, local_start, tok_rows)
    my_segment = lax.dynamic_slice_in_dim(segment_id, local_start, tok_rows)
    my_position = lax.dynamic_slice_in_dim(position, local_start, tok_rows)
    allowed = (my_segment[:, None] == segment_id[None, :]) & (
        packed_pos[None, :] <= my_packed[:, None]
    )
    allowed_cols = (segment_id[:, None] == my_segment[None, :]) & (
        my_packed[None, :] <= packed_pos[:, None]
    )
    return (my_position, allowed, allowed_cols)


def rotary_tables(position, rotary_dims):
    pair_index = jnp.arange(rotary_dims // 2, dtype=jnp.float32)
    inverse = jnp.power(10000.0, -2.0 * pair_index / rotary_dims)
    angles = position.astype(jnp.float32)[:, None] * inverse[None, :]
    return (jnp.cos(angles), jnp.sin(angles))


def rotate(values, cosine_table, sine_table, rotary_dims):
    half_dim = rotary_dims // 2
    first_half = values[..., :half_dim]
    second_half = values[..., half_dim:rotary_dims]
    remainder = values[..., rotary_dims:]
    cosine = cosine_table[:, None, :]
    sine_part = sine_table[:, None, :]
    return jnp.concatenate(
        [
            first_half * cosine - second_half * sine_part,
            second_half * cosine + first_half * sine_part,
            remainder,
        ],
        axis=-1,
    )


def unrotate(values, cosine_table, sine_table, rotary_dims):
    half_dim = rotary_dims // 2
    first_half = values[..., :half_dim]
    second_half = values[..., half_dim:rotary_dims]
    remainder = values[..., rotary_dims:]
    cosine = cosine_table[:, None, :]
    sine_part = sine_table[:, None, :]
    return jnp.concatenate(
        [
            first_half * cosine + second_half * sine_part,
            second_half * cosine - first_half * sine_part,
            remainder,
        ],
        axis=-1,
    )


def normalize(values, norm_gain, norm_bias):
    average = jnp.mean(values, axis=-1, keepdims=True)
    centered = values - average
    inv_std = lax.rsqrt(jnp.mean(centered * centered, axis=-1, keepdims=True) + EPSILON)
    scaled = centered * inv_std
    return (scaled * norm_gain + norm_bias, scaled, inv_std)


def norm_backward(grad_normed, scaled, inv_std, norm_gain):
    grad_scaled = grad_normed * norm_gain
    grad_values = inv_std * (
        grad_scaled
        - jnp.mean(grad_scaled, axis=-1, keepdims=True)
        - scaled * jnp.mean(grad_scaled * scaled, axis=-1, keepdims=True)
    )
    return (grad_values, jnp.sum(grad_normed * scaled, axis=0), jnp.sum(grad_normed, axis=0))


def gelu_slope(values):
    return (
        0.5 * (1.0 + lax.erf(values * 0.7071067811865476))
        + values * jnp.exp(-0.5 * values * values) * 0.3989422804014327
    )


def bias_keep(width):
    feature = jnp.arange(width, dtype=jnp.int32) % HD
    part_index = jnp.arange(3, dtype=jnp.int32)[:, None]
    return jnp.where((part_index == 1) & (feature[None, :] >= ROT), 0.0, 1.0).astype(jnp.float32)


def gather_weights(shards):
    return (
        lax.all_gather(shards[0], CTX, axis=0, tiled=True),
        lax.all_gather(shards[1], CTX, axis=0, tiled=True),
        lax.all_gather(shards[2], CTX, axis=0, tiled=True),
        lax.all_gather(shards[3], CTX, axis=0, tiled=True),
        lax.all_gather(shards[4], CTX, axis=1, tiled=True),
        lax.all_gather(shards[5], CTX, axis=1, tiled=True),
        lax.all_gather(shards[6], CTX, axis=1, tiled=True),
        lax.all_gather(shards[7], CTX, axis=0, tiled=True),
        lax.all_gather(shards[8], CTX, axis=0, tiled=True),
        lax.all_gather(shards[9], CTX, axis=0, tiled=True),
        lax.all_gather(shards[10], CTX, axis=1, tiled=True),
        lax.all_gather(shards[11], CTX, axis=0, tiled=True),
    )


def split_pairs(pair_all, local_heads):
    total_rows = pair_all.shape[0]
    local_width = pair_all.shape[1] // 2
    keys_all = pair_all[:, :local_width].reshape(total_rows, local_heads, HD)
    vals_all = pair_all[:, local_width:].reshape(total_rows, local_heads, HD)
    return (keys_all, vals_all)


def attention_forward(queries, pair_all, allowed):
    keys_all, vals_all = split_pairs(pair_all, queries.shape[1])
    scale_factor = HD ** (-0.5)
    scores = (
        jnp.einsum("qhd,khd->hqk", queries, keys_all, preferred_element_type=jnp.float32)
        * scale_factor
    )
    scores = jnp.where(allowed[None], scores, MASKED)
    row_peak = jnp.max(scores, axis=2, keepdims=True)
    exp_scores = jnp.exp(scores - row_peak)
    row_total = jnp.sum(exp_scores, axis=2, keepdims=True)
    attn_probs = exp_scores / row_total
    log_total = row_peak[..., 0] + jnp.log(row_total[..., 0])
    attended = jnp.einsum(
        "hqk,khd->qhd",
        attn_probs.astype(jnp.bfloat16),
        vals_all,
        preferred_element_type=jnp.float32,
    )
    return (attended, log_total)


def attention_backward(queries, pair_all, log_total, attn_out, grad_attn, allowed):
    tok_rows, local_heads = (queries.shape[0], queries.shape[1])
    total_rows = pair_all.shape[0]
    local_width = local_heads * HD
    keys_all, vals_all = split_pairs(pair_all, local_heads)
    scale_factor = HD ** (-0.5)
    scores = (
        jnp.einsum("qhd,khd->hqk", queries, keys_all, preferred_element_type=jnp.float32)
        * scale_factor
    )
    scores = jnp.where(allowed[None], scores, MASKED)
    attn_probs = jnp.exp(scores - log_total[:, :, None])
    grad_heads = grad_attn.reshape(tok_rows, local_heads, HD)
    row_delta = jnp.sum(
        grad_heads.astype(jnp.float32)
        * attn_out.reshape(tok_rows, local_heads, HD).astype(jnp.float32),
        axis=2,
    )
    grad_probs = jnp.einsum(
        "qhd,khd->hqk", grad_heads, vals_all, preferred_element_type=jnp.float32
    )
    grad_scores = (attn_probs * (grad_probs - jnp.transpose(row_delta)[:, :, None])).astype(
        jnp.bfloat16
    )
    grad_query = (
        jnp.einsum("hqk,khd->qhd", grad_scores, keys_all, preferred_element_type=jnp.float32)
        * scale_factor
    )
    probs_rounded = attn_probs.astype(jnp.bfloat16)
    grad_keys = (
        jnp.einsum("hqk,qhd->khd", grad_scores, queries, preferred_element_type=jnp.float32)
        * scale_factor
    )
    grad_vals = jnp.einsum(
        "hqk,qhd->khd", probs_rounded, grad_heads, preferred_element_type=jnp.float32
    )
    key_terms = jnp.concatenate(
        [grad_keys.reshape(total_rows, local_width), grad_vals.reshape(total_rows, local_width)],
        axis=1,
    )
    own_rows = lax.psum_scatter(key_terms, CTX, scatter_dimension=0, tiled=True)
    return (
        grad_query,
        own_rows[:, :local_width].reshape(tok_rows, local_heads, HD),
        own_rows[:, local_width:],
    )


def layer_forward(hidden, weights, my_position, allowed):
    (
        norm1_gain,
        norm1_bias,
        norm2_gain,
        norm2_bias,
        qkv_w,
        qkv_b,
        dense_w,
        dense_b,
        up_w,
        up_b,
        down_w,
        down_b,
    ) = weights
    tok_rows = hidden.shape[0]
    local_width = qkv_w.shape[2]
    local_heads = local_width // HD
    hidden_wide = hidden.astype(jnp.float32)
    normed_one, scaled_one, inv_std_one = normalize(
        hidden_wide, norm1_gain.astype(jnp.float32), norm1_bias.astype(jnp.float32)
    )
    attn_input = normed_one.astype(jnp.bfloat16)
    mlp_input = (
        scaled_one * norm2_gain.astype(jnp.float32) + norm2_bias.astype(jnp.float32)
    ).astype(jnp.bfloat16)
    projected = (
        jnp.einsum("td,cde->cte", attn_input, qkv_w, preferred_element_type=jnp.float32)
        + qkv_b.astype(jnp.float32)[:, None, :]
    )
    cosine_table, sine_table = rotary_tables(my_position, ROT)
    queries = rotate(
        projected[0].reshape(tok_rows, local_heads, HD), cosine_table, sine_table, ROT
    ).astype(jnp.bfloat16)
    key_rows = rotate(
        projected[1].reshape(tok_rows, local_heads, HD), cosine_table, sine_table, ROT
    ).astype(jnp.bfloat16)
    value_rows = projected[2].astype(jnp.bfloat16)
    pair_local = jnp.concatenate([key_rows.reshape(tok_rows, local_width), value_rows], axis=1)
    pair_all = lax.all_gather(pair_local, CTX, axis=0, tiled=True)
    attended, log_total = attention_forward(queries, pair_all, allowed)
    attn_out = attended.reshape(tok_rows, local_width).astype(jnp.bfloat16)
    up_linear = jnp.dot(mlp_input, up_w, preferred_element_type=jnp.float32) + up_b.astype(
        jnp.float32
    )
    act_rounded = jax.nn.gelu(up_linear, approximate=False).astype(jnp.bfloat16)
    branch_terms = jnp.dot(attn_out, dense_w, preferred_element_type=jnp.float32) + jnp.dot(
        act_rounded, down_w, preferred_element_type=jnp.float32
    )
    summed = lax.psum(branch_terms, TEN)
    output = (
        hidden_wide + summed + dense_b.astype(jnp.float32) + down_b.astype(jnp.float32)
    ).astype(jnp.bfloat16)
    kept_state = (hidden, queries, pair_local, log_total, attn_out, up_linear, pair_all)
    return (output, kept_state)


def layer_backward(kept_state, cotangent, weights, my_position, allowed):
    (
        norm1_gain,
        norm1_bias,
        norm2_gain,
        norm2_bias,
        qkv_w,
        qkv_b,
        dense_w,
        dense_b,
        up_w,
        up_b,
        down_w,
        down_b,
    ) = weights
    hidden, queries, pair_local, log_total, attn_out, up_linear = (
        kept_state[0],
        kept_state[1],
        kept_state[2],
        kept_state[3],
        kept_state[4],
        kept_state[5],
    )
    pair_all = kept_state[6]
    tok_rows = hidden.shape[0]
    local_width = qkv_w.shape[2]
    hidden_wide = hidden.astype(jnp.float32)
    normed_one, scaled_one, inv_std_one = normalize(
        hidden_wide, norm1_gain.astype(jnp.float32), norm1_bias.astype(jnp.float32)
    )
    attn_input = normed_one.astype(jnp.bfloat16)
    mlp_input = (
        scaled_one * norm2_gain.astype(jnp.float32) + norm2_bias.astype(jnp.float32)
    ).astype(jnp.bfloat16)
    cot_wide = cotangent.astype(jnp.float32)
    act_rounded = jax.nn.gelu(up_linear, approximate=False).astype(jnp.bfloat16)
    grad_down_w = jnp.einsum(
        "tf,td->fd", act_rounded, cotangent, preferred_element_type=jnp.float32
    )
    grad_act = jnp.einsum("td,fd->tf", cotangent, down_w, preferred_element_type=jnp.float32)
    grad_up = grad_act * gelu_slope(up_linear)
    grad_up_bf = grad_up.astype(jnp.bfloat16)
    grad_up_w = jnp.einsum("td,tf->df", mlp_input, grad_up_bf, preferred_element_type=jnp.float32)
    grad_mlp = jnp.einsum("tf,df->td", grad_up_bf, up_w, preferred_element_type=jnp.float32)
    grad_dense_w = jnp.einsum("te,td->ed", attn_out, cotangent, preferred_element_type=jnp.float32)
    grad_attn = jnp.einsum(
        "td,ed->te", cotangent, dense_w, preferred_element_type=jnp.float32
    ).astype(jnp.bfloat16)
    grad_query, grad_keys, grad_vals = attention_backward(
        queries, pair_all, log_total, attn_out, grad_attn, allowed
    )
    cosine_table, sine_table = rotary_tables(my_position, ROT)
    grad_query = unrotate(grad_query, cosine_table, sine_table, ROT).reshape(tok_rows, local_width)
    grad_keys = unrotate(grad_keys, cosine_table, sine_table, ROT).reshape(tok_rows, local_width)
    grad_proj = jnp.stack([grad_query, grad_keys, grad_vals])
    grad_proj_bf = grad_proj.astype(jnp.bfloat16)
    grad_qkv_w = jnp.einsum(
        "td,cte->cde", attn_input, grad_proj_bf, preferred_element_type=jnp.float32
    )
    grad_attn_in = jnp.einsum(
        "cte,cde->td", grad_proj_bf, qkv_w, preferred_element_type=jnp.float32
    )
    grad_attn_in, grad_mlp = lax.psum((grad_attn_in, grad_mlp), TEN)
    grad_one, gain_one, shift_one = norm_backward(
        grad_attn_in, scaled_one, inv_std_one, norm1_gain.astype(jnp.float32)
    )
    grad_two, gain_two, shift_two = norm_backward(
        grad_mlp, scaled_one, inv_std_one, norm2_gain.astype(jnp.float32)
    )
    grad_hidden = (cot_wide + grad_one + grad_two).astype(jnp.bfloat16)
    bias_sum = jnp.sum(cot_wide, axis=0)
    qkv_bias_sum = jnp.sum(grad_proj, axis=1) * bias_keep(local_width)
    layer_grads = (
        gain_one,
        shift_one,
        gain_two,
        shift_two,
        grad_qkv_w,
        qkv_bias_sum,
        grad_dense_w,
        bias_sum,
        grad_up_w,
        jnp.sum(grad_up, axis=0),
        grad_down_w,
        bias_sum,
    )
    return (grad_hidden, layer_grads)


def body(
    layer_input,
    out_cotangent,
    seq_lengths,
    block_order,
    ln1_gain,
    ln1_bias,
    ln2_gain,
    ln2_bias,
    qkv_weight,
    qkv_bias,
    dense_weight,
    dense_bias,
    up_weight,
    up_bias,
    down_weight,
    down_bias,
):
    section_index = lax.axis_index(SEC)
    context_index = lax.axis_index(CTX)
    micro_count = layer_input.shape[0]
    tok_rows = layer_input.shape[1]
    block_rows = tok_rows // 2
    shards = (
        ln1_gain[0],
        ln1_bias[0],
        ln2_gain[0],
        ln2_bias[0],
        qkv_weight[0],
        qkv_bias[0],
        dense_weight[0],
        dense_bias[0],
        up_weight[0],
        up_bias[0],
        down_weight[0],
        down_bias[0],
    )
    forward_outs = []
    state_list = []
    incoming = jnp.zeros_like(layer_input[0])
    for tick_index in range(micro_count + 1):
        micro_index = jnp.clip(tick_index - section_index, 0, micro_count - 1)
        hidden = jnp.where(
            section_index == 0, layer_input[min(tick_index, micro_count - 1)], incoming
        )
        weights = gather_weights(shards)
        my_position, allowed, allowed_cols = micro_layout(
            seq_lengths, block_order, micro_index, block_rows, context_index, tok_rows
        )
        output, kept_state = layer_forward(hidden, weights, my_position, allowed)
        forward_outs.append(output)
        state_list.append(kept_state)
        if tick_index < micro_count:
            incoming = shifted(output, SEC, 1)
    stacked_outs = jnp.stack(forward_outs)
    layer_out = jnp.where(section_index == 0, stacked_outs[:micro_count], stacked_outs[1:])
    state_stack = jax.tree.map(lambda *leaves: jnp.stack(leaves), *state_list)
    grad_totals = None
    backward_outs = []
    incoming_grad = jnp.zeros_like(out_cotangent[0])
    for tick_index in range(micro_count + 1):
        micro_raw = tick_index - 1 + section_index
        is_valid = (micro_raw >= 0) & (micro_raw < micro_count)
        micro_index = jnp.clip(micro_raw, 0, micro_count - 1)
        state_index = jnp.clip(micro_raw + section_index, 0, micro_count)
        kept_state = jax.tree.map(
            lambda leaf_array: lax.dynamic_index_in_dim(leaf_array, state_index, 0, keepdims=False),
            state_stack,
        )
        cotangent = jnp.where(
            section_index == 1, out_cotangent[min(tick_index, micro_count - 1)], incoming_grad
        )
        weights = gather_weights(shards)
        my_position, allowed, allowed_cols = micro_layout(
            seq_lengths, block_order, micro_index, block_rows, context_index, tok_rows
        )
        grad_hidden, layer_grads = layer_backward(
            kept_state, cotangent, weights, my_position, allowed
        )
        layer_grads = jax.tree.map(
            lambda leaf_array: jnp.where(is_valid, leaf_array, 0.0), layer_grads
        )
        grad_totals = (
            layer_grads if grad_totals is None else jax.tree.map(jnp.add, grad_totals, layer_grads)
        )
        backward_outs.append(grad_hidden)
        if tick_index < micro_count:
            incoming_grad = shifted(grad_hidden, SEC, -1)
    stacked_grads = jnp.stack(backward_outs)
    input_grad = jnp.where(section_index == 1, stacked_grads[:micro_count], stacked_grads[1:])
    owned_grads = (
        lax.psum_scatter(
            grad_totals[0].astype(jnp.bfloat16), CTX, scatter_dimension=0, tiled=True
        ).astype(jnp.float32),
        lax.psum_scatter(
            grad_totals[1].astype(jnp.bfloat16), CTX, scatter_dimension=0, tiled=True
        ).astype(jnp.float32),
        lax.psum_scatter(
            grad_totals[2].astype(jnp.bfloat16), CTX, scatter_dimension=0, tiled=True
        ).astype(jnp.float32),
        lax.psum_scatter(
            grad_totals[3].astype(jnp.bfloat16), CTX, scatter_dimension=0, tiled=True
        ).astype(jnp.float32),
        lax.psum_scatter(
            grad_totals[4].astype(jnp.bfloat16), CTX, scatter_dimension=1, tiled=True
        ).astype(jnp.float32),
        lax.psum_scatter(
            grad_totals[5].astype(jnp.bfloat16), CTX, scatter_dimension=1, tiled=True
        ).astype(jnp.float32),
        lax.psum_scatter(
            grad_totals[6].astype(jnp.bfloat16), CTX, scatter_dimension=1, tiled=True
        ).astype(jnp.float32),
        lax.psum_scatter(
            grad_totals[7].astype(jnp.bfloat16), CTX, scatter_dimension=0, tiled=True
        ).astype(jnp.float32),
        lax.psum_scatter(
            grad_totals[8].astype(jnp.bfloat16), CTX, scatter_dimension=0, tiled=True
        ).astype(jnp.float32),
        lax.psum_scatter(
            grad_totals[9].astype(jnp.bfloat16), CTX, scatter_dimension=0, tiled=True
        ).astype(jnp.float32),
        lax.psum_scatter(
            grad_totals[10].astype(jnp.bfloat16), CTX, scatter_dimension=1, tiled=True
        ).astype(jnp.float32),
        lax.psum_scatter(
            grad_totals[11].astype(jnp.bfloat16), CTX, scatter_dimension=0, tiled=True
        ).astype(jnp.float32),
    )
    return (
        layer_out[None],
        input_grad[None],
        owned_grads[0][None],
        owned_grads[1][None],
        owned_grads[2][None],
        owned_grads[3][None],
        owned_grads[4][None],
        owned_grads[5][None],
        owned_grads[6][None],
        owned_grads[7][None],
        owned_grads[8][None],
        owned_grads[9][None],
        owned_grads[10][None],
        owned_grads[11][None],
    )


def wide_attention(queries, keys, vals, allowed):
    scores = jnp.einsum("qhd,khd->hqk", queries, keys, preferred_element_type=jnp.float32)
    scores = jnp.where(allowed[None], scores * HD ** (-0.5), MASKED)
    row_peak = jnp.max(scores, axis=2, keepdims=True)
    exp_scores = jnp.exp(scores - row_peak)
    probs = exp_scores / jnp.sum(exp_scores, axis=2, keepdims=True)
    attended = jnp.einsum(
        "hqk,khd->qhd", probs.astype(jnp.bfloat16), vals, preferred_element_type=jnp.float32
    )
    return (attended, probs)


def sum_kernel(sizes, backward, last, *refs):
    tensors, contexts = sizes
    count = tensors * contexts
    refs = list(refs)
    parts = refs.pop(0)
    base = refs.pop(0)
    scaled, inv = (refs.pop(0), refs.pop(0)) if backward else (None, None)
    vec = refs.pop(0) if last else None
    out = refs.pop(0)
    vec_out = refs.pop(0) if last else None
    landed, send1, recv1, send2, recv2 = (refs.pop(0) for _ in range(5))
    vec_landed, vec_send, vec_recv = refs if last else (None, None, None)
    tensor = lax.axis_index(TEN)
    context = lax.axis_index(CTX)
    me = context * tensors + tensor

    def device(peer):
        return {TEN: lax.rem(peer, tensors), CTX: lax.div(peer, tensors)}

    def ahead(k):
        return lax.rem(me + k, count)

    def behind(k):
        return lax.rem(me + count - k, count)

    def copy_part(k, peer, slot):
        return pltpu.make_async_remote_copy(
            src_ref=parts.at[peer],
            dst_ref=landed.at[slot],
            send_sem=send1.at[k],
            recv_sem=recv1.at[slot],
            device_id=device(peer),
            device_id_type=pl.DeviceIdType.MESH,
        )

    def copy_vec(k, peer, slot):
        return pltpu.make_async_remote_copy(
            src_ref=vec.at[lax.div(peer, tensors)],
            dst_ref=vec_landed.at[slot],
            send_sem=vec_send.at[k],
            recv_sem=vec_recv.at[slot],
            device_id=device(peer),
            device_id_type=pl.DeviceIdType.MESH,
        )

    barrier = pltpu.get_barrier_semaphore()

    @pl.loop(1, count)
    def _(k):
        pl.semaphore_signal(
            barrier, inc=1, device_id=device(ahead(k)), device_id_type=pl.DeviceIdType.MESH
        )

    pl.semaphore_wait(barrier, count - 1)

    @pl.loop(1, count)
    def _(k):
        copy_part(k, ahead(k), me).start()
        if last:
            copy_vec(k, ahead(k), me).start()

    def add(k, total):
        source = behind(k)
        copy_part(k, source, source).wait_recv()
        return total + landed[source].astype(jnp.float32)

    total = lax.fori_loop(1, count, add, parts[me].astype(jnp.float32))
    if backward:
        xhat = scaled[...]
        total = inv[...] * (
            total
            - jnp.mean(total, axis=-1, keepdims=True)
            - xhat * jnp.mean(total * xhat, axis=-1, keepdims=True)
        )
    own_slot = tensor if last else me
    out[own_slot] = (base[...] + total).astype(out.dtype)
    members = tensors if last else count

    def copy_out(k, step, slot):
        if last:
            peer = context * tensors + lax.rem(tensor + step, tensors)
        else:
            peer = lax.rem(me + step, count)
        return pltpu.make_async_remote_copy(
            src_ref=out.at[own_slot],
            dst_ref=out.at[slot],
            send_sem=send2.at[k],
            recv_sem=recv2.at[slot],
            device_id=device(peer),
            device_id_type=pl.DeviceIdType.MESH,
        )

    @pl.loop(1, members)
    def _(k):
        copy_out(k, k, own_slot).start()

    if last:

        def add_vec(k, rows):
            source = behind(k)
            copy_vec(k, source, source).wait_recv()
            return rows + vec_landed[source]

        vec_out[...] = lax.fori_loop(1, count, add_vec, vec[context])

    @pl.loop(1, members)
    def _(k):
        slot = lax.rem(own_slot + members - k, members)
        copy_out(k, members - k, slot).wait_recv()

    @pl.loop(1, members)
    def _(k):
        copy_out(k, k, own_slot).wait_send()

    @pl.loop(1, count)
    def _(k):
        copy_part(k, ahead(k), me).wait_send()
        if last:
            copy_vec(k, ahead(k), me).wait_send()


def own_rows(x, rows):
    tensors = lax.axis_size(TEN)
    start = (lax.axis_index(CTX) * tensors + lax.axis_index(TEN)) * rows
    return lax.dynamic_slice_in_dim(x, start, rows, 0)


def sum_rows(parts, base, call_id, norm=(), vec=None):
    sizes = (lax.axis_size(TEN), lax.axis_size(CTX))
    count = sizes[0] * sizes[1]
    total_rows, features = parts.shape
    rows = total_rows // count
    last = vec is not None
    members = sizes[0] if last else count
    f32, bf16 = jnp.float32, jnp.bfloat16
    operands = [parts.astype(bf16).reshape(count, rows, features), own_rows(base, rows), *norm]
    outs = [jax.ShapeDtypeStruct((members, rows, features), bf16)]
    scratch = [pltpu.VMEM((count, rows, features), bf16)]
    scratch += [pltpu.SemaphoreType.DMA((count,))] * 4
    if last:
        operands.append(vec)
        outs.append(jax.ShapeDtypeStruct(vec.shape[1:], f32))
        scratch.append(pltpu.VMEM((count, *vec.shape[1:]), f32))
        scratch += [pltpu.SemaphoreType.DMA((count,))] * 2
    spec = pl.BlockSpec(memory_space=pltpu.VMEM)
    results = pl.pallas_call(
        functools.partial(sum_kernel, sizes, bool(norm), last),
        out_shape=outs,
        in_specs=[spec] * len(operands),
        out_specs=[spec] * len(outs),
        scratch_shapes=scratch,
        compiler_params=pltpu.CompilerParams(collective_id=call_id, has_side_effects=True),
    )(*operands)
    return (results[0].reshape(members * rows, features), *results[1:])


def wide_forward(hidden, weights, tables, allowed, call_id):
    gain1, bias1, gain2, bias2, dense_b, down_b, qkv_w, qkv_b, dense_w, up_w, up_b, down_w = weights
    rows = hidden.shape[0]
    width = qkv_w.shape[2]
    heads = width // HD
    hidden_wide = hidden.astype(jnp.float32)
    normed, scaled, inv_std = normalize(hidden_wide, gain1, bias1)
    attn_input = normed.astype(jnp.bfloat16)
    mlp_input = (scaled * gain2 + bias2).astype(jnp.bfloat16)
    projected = (
        jnp.einsum("td,cde->cte", attn_input, qkv_w, preferred_element_type=jnp.float32)
        + qkv_b[:, None, :]
    )
    queries = rotate(projected[0].reshape(rows, heads, HD), *tables, ROT).astype(jnp.bfloat16)
    keys = rotate(projected[1].reshape(rows, heads, HD), *tables, ROT).astype(jnp.bfloat16)
    vals = projected[2].astype(jnp.bfloat16).reshape(rows, heads, HD)
    attended, probs = wide_attention(queries, keys, vals, allowed)
    attn_out = attended.reshape(rows, width).astype(jnp.bfloat16)
    up_linear = jnp.dot(mlp_input, up_w, preferred_element_type=jnp.float32) + up_b
    act = jax.nn.gelu(up_linear, approximate=False).astype(jnp.bfloat16)
    parts = jnp.dot(attn_out, dense_w, preferred_element_type=jnp.float32) + jnp.dot(
        act, down_w, preferred_element_type=jnp.float32
    )
    (output,) = sum_rows(parts, hidden_wide + (dense_b + down_b), call_id)
    state = (attn_input, mlp_input, scaled, inv_std, queries, keys, vals, probs, attn_out, up_linear, act)
    return (output, state)


def wide_backward(state, cotangent, weights, tables, call_id, later):
    gain1, bias1, gain2, bias2, dense_b, down_b, qkv_w, qkv_b, dense_w, up_w, up_b, down_w = weights
    attn_input, mlp_input, scaled, inv_std, queries, keys, vals, probs, attn_out, up_linear, act = state
    rows = cotangent.shape[0]
    width = qkv_w.shape[2]
    heads = width // HD
    f32 = jnp.float32
    cot_wide = cotangent.astype(f32)
    grad_act = jnp.einsum("td,fd->tf", cotangent, down_w, preferred_element_type=f32)
    grad_up = grad_act * gelu_slope(up_linear)
    grad_up_bf = grad_up.astype(jnp.bfloat16)
    grad_attn = jnp.einsum("td,ed->te", cotangent, dense_w, preferred_element_type=f32).astype(
        jnp.bfloat16
    )
    grad_heads = grad_attn.reshape(rows, heads, HD)
    delta = jnp.sum(
        grad_heads.astype(f32) * attn_out.reshape(rows, heads, HD).astype(f32), axis=2
    )
    grad_probs = jnp.einsum("qhd,khd->hqk", grad_heads, vals, preferred_element_type=f32)
    grad_scores = (probs * (grad_probs - jnp.transpose(delta)[:, :, None])).astype(jnp.bfloat16)
    scale = HD ** (-0.5)
    grad_q = jnp.einsum("hqk,khd->qhd", grad_scores, keys, preferred_element_type=f32) * scale
    grad_k = jnp.einsum("hqk,qhd->khd", grad_scores, queries, preferred_element_type=f32) * scale
    grad_v = jnp.einsum(
        "hqk,qhd->khd", probs.astype(jnp.bfloat16), grad_heads, preferred_element_type=f32
    )
    grad_proj = jnp.stack(
        [
            unrotate(grad_q, *tables, ROT).reshape(rows, width),
            unrotate(grad_k, *tables, ROT).reshape(rows, width),
            grad_v.reshape(rows, width),
        ]
    )
    grad_proj_bf = grad_proj.astype(jnp.bfloat16)
    grad_a1 = jnp.einsum("cte,cde->td", grad_proj_bf, qkv_w, preferred_element_type=f32)
    grad_a2 = jnp.einsum("tf,df->td", grad_up_bf, up_w, preferred_element_type=f32)
    shared = jnp.stack(
        [
            jnp.sum(grad_a1 * scaled, axis=0),
            jnp.sum(grad_a1, axis=0),
            jnp.sum(grad_a2 * scaled, axis=0),
            jnp.sum(grad_a2, axis=0),
        ]
    )
    first = (lax.axis_index(TEN) == 0) & (lax.axis_index(CTX) == 0)
    bias_sum = jnp.where(first, jnp.sum(cot_wide, axis=0), 0.0)
    shared = jnp.concatenate([shared, bias_sum[None]], axis=0)
    own = jnp.concatenate(
        [
            (jnp.sum(grad_proj, axis=1) * bias_keep(width)).reshape(-1),
            jnp.sum(grad_up, axis=0),
        ]
    )
    grad_w = (
        jnp.einsum("td,cte->cde", attn_input, grad_proj_bf, preferred_element_type=f32),
        jnp.einsum("te,td->ed", attn_out, cotangent, preferred_element_type=f32),
        jnp.einsum("td,tf->df", mlp_input, grad_up_bf, preferred_element_type=f32),
        jnp.einsum("tf,td->fd", act, cotangent, preferred_element_type=f32),
    )
    rows = rows // (lax.axis_size(TEN) * lax.axis_size(CTX))
    xhat = own_rows(scaled, rows)
    norm = (xhat, jnp.broadcast_to(own_rows(inv_std, rows), xhat.shape))
    vec = None
    if later is not None:
        vec = jnp.concatenate([shared, later, jnp.zeros((6, shared.shape[1]), f32)], axis=0)
        vec = vec.reshape(vec.shape[0], lax.axis_size(CTX), -1).swapaxes(0, 1)
    grad_hidden, *rest = sum_rows(
        grad_a1 * gain1 + grad_a2 * gain2, cot_wide, call_id, norm, vec
    )
    return (grad_hidden, rest[0] if rest else shared, own, grad_w)


def swap_sections(pair):
    section = lax.axis_index(SEC)
    theirs = lax.dynamic_index_in_dim(pair, 1 - section, 0, keepdims=False)
    mine = lax.dynamic_index_in_dim(pair, section, 0, keepdims=False)
    return (mine, lax.ppermute(theirs, SEC, [(0, 1), (1, 0)]))


def wide_body(
    layer_input,
    out_cotangent,
    seq_lengths,
    block_order,
    ln1_gain,
    ln1_bias,
    ln2_gain,
    ln2_bias,
    qkv_weight,
    qkv_bias,
    dense_weight,
    dense_bias,
    up_weight,
    up_bias,
    down_weight,
    down_bias,
):
    f32 = jnp.float32
    bf16 = jnp.bfloat16
    section = lax.axis_index(SEC)
    context = lax.axis_index(CTX)
    tok_rows = layer_input.shape[1]
    block_rows = tok_rows * lax.axis_size(CTX) // block_order.shape[1]
    edges = jnp.stack(
        [
            lax.dynamic_index_in_dim(layer_input, section, 0, keepdims=False),
            lax.dynamic_index_in_dim(out_cotangent, section, 0, keepdims=False),
        ]
    )
    edges = lax.all_gather(edges, CTX, axis=1, tiled=True)
    vectors = jnp.concatenate([ln1_gain, ln1_bias, ln2_gain, ln2_bias, dense_bias, down_bias], axis=0)
    vectors = lax.all_gather(
        lax.all_gather(vectors, CTX, axis=1, tiled=True), SEC, axis=0
    ).astype(f32)
    own_bias = lax.all_gather(
        jnp.concatenate([qkv_bias[0].reshape(-1), up_bias[0]]), SEC, axis=0
    ).astype(f32)
    width = qkv_bias.shape[2]
    matrices = (
        lax.all_to_all(qkv_weight[0], CTX, 2, 1, tiled=True),
        lax.all_to_all(dense_weight[0], CTX, 0, 1, tiled=True),
        lax.all_to_all(up_weight[0], CTX, 1, 0, tiled=True),
        lax.all_to_all(down_weight[0], CTX, 0, 1, tiled=True),
    )
    matrices = tuple(lax.all_gather(leaf, SEC, axis=0) for leaf in matrices)
    weights = [
        (
            *(vectors[layer, i] for i in range(6)),
            matrices[0][layer],
            own_bias[layer, : 3 * width].reshape(3, width),
            matrices[1][layer],
            matrices[2][layer],
            own_bias[layer, 3 * width :],
            matrices[3][layer],
        )
        for layer in range(2)
    ]
    lengths = lax.dynamic_index_in_dim(seq_lengths, section, 0, keepdims=False)
    perm = lax.dynamic_index_in_dim(block_order, section, 0, keepdims=False)
    packed_pos, segment_id, position = packed_layout(lengths, perm, block_rows)
    allowed = (segment_id[:, None] == segment_id[None, :]) & (
        packed_pos[None, :] <= packed_pos[:, None]
    )
    tables = rotary_tables(position, ROT)
    hidden = edges[0]
    states = []
    outs = []
    for layer in range(2):
        hidden, state = wide_forward(hidden, weights[layer], tables, allowed, layer)
        outs.append(hidden)
        states.append(state)
    cotangent = edges[1]
    grads = [None, None]
    cots = [None, None]
    for layer in (1, 0):
        cotangent, shared, own, grad_w = wide_backward(
            states[layer],
            cotangent,
            weights[layer],
            tables,
            2 + layer,
            None if layer else grads[1][0],
        )
        cots[layer] = cotangent
        grads[layer] = (shared, own, grad_w)
    local = [
        lax.dynamic_slice_in_dim(rows, context * tok_rows, tok_rows, 0)
        for rows in (outs[0], outs[1], cots[1])
    ]
    both = jnp.stack([jnp.stack([local[0], cots[0]]), jnp.stack([local[1], local[2]])])
    mine, theirs = swap_sections(both)
    low = jnp.where(section == 0, mine, theirs)
    high = jnp.where(section == 0, theirs, mine)
    layer_out = jnp.stack([low[0], high[0]])
    input_grad = jnp.stack([low[1], high[1]])
    vec = grads[0][0][:10].reshape(2, -1)
    own = jnp.stack([grads[0][1], grads[1][1]])
    mine, theirs = swap_sections(jnp.concatenate([vec, own], axis=1))
    own = mine + theirs
    shared = own[: vec.shape[1]].reshape(5, -1)
    own = own[vec.shape[1] :]
    summed = []
    for i in range(4):
        pair = jnp.stack([grads[0][2][i], grads[1][2][i]])
        mine = lax.dynamic_index_in_dim(pair, section, 0, keepdims=False)
        theirs = lax.dynamic_index_in_dim(pair, 1 - section, 0, keepdims=False).astype(bf16)
        summed.append(
            (mine + lax.ppermute(theirs, SEC, [(0, 1), (1, 0)]).astype(f32)).astype(bf16)
        )
    qkv_g = lax.all_to_all(summed[0], CTX, 1, 2, tiled=True).astype(f32)
    dense_g = lax.all_to_all(summed[1], CTX, 1, 0, tiled=True).astype(f32)
    up_g = lax.all_to_all(summed[2], CTX, 0, 1, tiled=True).astype(f32)
    down_g = lax.all_to_all(summed[3], CTX, 1, 0, tiled=True).astype(f32)
    return (
        layer_out[None],
        input_grad[None],
        shared[0][None],
        shared[1][None],
        shared[2][None],
        shared[3][None],
        qkv_g[None],
        own[: 3 * width].reshape(1, 3, width),
        dense_g[None],
        shared[4][None],
        up_g[None],
        own[3 * width :][None],
        down_g[None],
        shared[4][None],
    )


def plan(*args):
    heads = args[10].shape[1] // HD
    units = lax.axis_size(CTX)
    count = units * lax.axis_size(TEN)
    tiled = args[0].shape[1] * units % (16 * count) == 0
    if heads % units == 0 and tiled and args[0].shape[0] == lax.axis_size(SEC) == 2:
        return wide_body(*args)
    return body(*args)


def solution(mesh):
    return jax.shard_map(
        plan,
        mesh=mesh,
        in_specs=(
            P(None, CTX, None),
            P(None, CTX, None),
            P(),
            P(),
            P(SEC, CTX),
            P(SEC, CTX),
            P(SEC, CTX),
            P(SEC, CTX),
            P(SEC, None, CTX, TEN),
            P(SEC, None, (TEN, CTX)),
            P(SEC, TEN, CTX),
            P(SEC, CTX),
            P(SEC, CTX, TEN),
            P(SEC, (TEN, CTX)),
            P(SEC, TEN, CTX),
            P(SEC, CTX),
        ),
        out_specs=(
            P(SEC, None, CTX, None),
            P(SEC, None, CTX, None),
            P(SEC, CTX),
            P(SEC, CTX),
            P(SEC, CTX),
            P(SEC, CTX),
            P(SEC, None, CTX, TEN),
            P(SEC, None, (TEN, CTX)),
            P(SEC, TEN, CTX),
            P(SEC, CTX),
            P(SEC, CTX, TEN),
            P(SEC, (TEN, CTX)),
            P(SEC, TEN, CTX),
            P(SEC, CTX),
        ),
        check_vma=False,
    )
```

```python
import functools
import math

import jax
import jax.numpy as jnp
from jax import lax
from jax.experimental import pallas as pl
from jax.experimental.pallas import tpu as pltpu
from jax.sharding import PartitionSpec as P

CTX = "context"
TEN = "tensor"
SEC = "section"
HD = 64
ROT = 16


EPSILON = 1e-05
MASKED = -1e30


def shifted(x, axis, by):
    count = lax.axis_size(axis)
    pairs = [(i, i + by) for i in range(count) if 0 <= i + by < count]
    return lax.ppermute(x, axis, pairs)


def packed_layout(lengths, block_perm, block_rows):
    total_rows = block_perm.shape[0] * block_rows
    row_index = jnp.arange(total_rows, dtype=jnp.int32)
    chosen = (row_index // block_rows)[:, None] == jnp.arange(block_perm.shape[0], dtype=jnp.int32)[
        None, :
    ]
    packed_pos = (
        jnp.sum(jnp.where(chosen, block_perm[None, :], 0), axis=1) * block_rows
        + row_index % block_rows
    )
    seq_ends = jnp.cumsum(lengths)
    passed = seq_ends[None, :] <= packed_pos[:, None]
    segment_id = jnp.sum(passed.astype(jnp.int32), axis=1)
    seq_start = jnp.sum(jnp.where(passed, lengths[None, :], 0), axis=1)
    return (packed_pos, segment_id, packed_pos - seq_start)


def micro_layout(seq_lengths, block_order, micro_index, block_rows, context_index, tok_rows):
    lengths = lax.dynamic_index_in_dim(seq_lengths, micro_index, 0, keepdims=False)
    block_perm = lax.dynamic_index_in_dim(block_order, micro_index, 0, keepdims=False)
    packed_pos, segment_id, position = packed_layout(lengths, block_perm, block_rows)
    local_start = context_index * tok_rows
    my_packed = lax.dynamic_slice_in_dim(packed_pos, local_start, tok_rows)
    my_segment = lax.dynamic_slice_in_dim(segment_id, local_start, tok_rows)
    my_position = lax.dynamic_slice_in_dim(position, local_start, tok_rows)
    allowed = (my_segment[:, None] == segment_id[None, :]) & (
        packed_pos[None, :] <= my_packed[:, None]
    )
    allowed_cols = (segment_id[:, None] == my_segment[None, :]) & (
        my_packed[None, :] <= packed_pos[:, None]
    )
    return (my_position, allowed, allowed_cols)


def rotary_tables(position, rotary_dims):
    pair_index = jnp.arange(rotary_dims // 2, dtype=jnp.float32)
    inverse = jnp.power(10000.0, -2.0 * pair_index / rotary_dims)
    angles = position.astype(jnp.float32)[:, None] * inverse[None, :]
    return (jnp.cos(angles), jnp.sin(angles))


def rotate(values, cosine_table, sine_table, rotary_dims):
    half_dim = rotary_dims // 2
    first_half = values[..., :half_dim]
    second_half = values[..., half_dim:rotary_dims]
    remainder = values[..., rotary_dims:]
    cosine = cosine_table[:, None, :]
    sine_part = sine_table[:, None, :]
    return jnp.concatenate(
        [
            first_half * cosine - second_half * sine_part,
            second_half * cosine + first_half * sine_part,
            remainder,
        ],
        axis=-1,
    )


def unrotate(values, cosine_table, sine_table, rotary_dims):
    half_dim = rotary_dims // 2
    first_half = values[..., :half_dim]
    second_half = values[..., half_dim:rotary_dims]
    remainder = values[..., rotary_dims:]
    cosine = cosine_table[:, None, :]
    sine_part = sine_table[:, None, :]
    return jnp.concatenate(
        [
            first_half * cosine + second_half * sine_part,
            second_half * cosine - first_half * sine_part,
            remainder,
        ],
        axis=-1,
    )


def normalize(values, norm_gain, norm_bias):
    average = jnp.mean(values, axis=-1, keepdims=True)
    centered = values - average
    inv_std = lax.rsqrt(jnp.mean(centered * centered, axis=-1, keepdims=True) + EPSILON)
    scaled = centered * inv_std
    return (scaled * norm_gain + norm_bias, scaled, inv_std)


def norm_backward(grad_normed, scaled, inv_std, norm_gain):
    grad_scaled = grad_normed * norm_gain
    grad_values = inv_std * (
        grad_scaled
        - jnp.mean(grad_scaled, axis=-1, keepdims=True)
        - scaled * jnp.mean(grad_scaled * scaled, axis=-1, keepdims=True)
    )
    return (grad_values, jnp.sum(grad_normed * scaled, axis=0), jnp.sum(grad_normed, axis=0))


def gelu_slope(values):
    return (
        0.5 * (1.0 + lax.erf(values * 0.7071067811865476))
        + values * jnp.exp(-0.5 * values * values) * 0.3989422804014327
    )


def bias_keep(width):
    feature = jnp.arange(width, dtype=jnp.int32) % HD
    part_index = jnp.arange(3, dtype=jnp.int32)[:, None]
    return jnp.where((part_index == 1) & (feature[None, :] >= ROT), 0.0, 1.0).astype(jnp.float32)


def gather_weights(shards):
    return (
        lax.all_gather(shards[0], CTX, axis=0, tiled=True),
        lax.all_gather(shards[1], CTX, axis=0, tiled=True),
        lax.all_gather(shards[2], CTX, axis=0, tiled=True),
        lax.all_gather(shards[3], CTX, axis=0, tiled=True),
        lax.all_gather(shards[4], CTX, axis=1, tiled=True),
        lax.all_gather(shards[5], CTX, axis=1, tiled=True),
        lax.all_gather(shards[6], CTX, axis=1, tiled=True),
        lax.all_gather(shards[7], CTX, axis=0, tiled=True),
        lax.all_gather(shards[8], CTX, axis=0, tiled=True),
        lax.all_gather(shards[9], CTX, axis=0, tiled=True),
        lax.all_gather(shards[10], CTX, axis=1, tiled=True),
        lax.all_gather(shards[11], CTX, axis=0, tiled=True),
    )


def split_pairs(pair_all, local_heads):
    total_rows = pair_all.shape[0]
    local_width = pair_all.shape[1] // 2
    keys_all = pair_all[:, :local_width].reshape(total_rows, local_heads, HD)
    vals_all = pair_all[:, local_width:].reshape(total_rows, local_heads, HD)
    return (keys_all, vals_all)


def attention_forward(queries, pair_all, allowed):
    keys_all, vals_all = split_pairs(pair_all, queries.shape[1])
    scale_factor = HD ** (-0.5)
    scores = (
        jnp.einsum("qhd,khd->hqk", queries, keys_all, preferred_element_type=jnp.float32)
        * scale_factor
    )
    scores = jnp.where(allowed[None], scores, MASKED)
    row_peak = jnp.max(scores, axis=2, keepdims=True)
    exp_scores = jnp.exp(scores - row_peak)
    row_total = jnp.sum(exp_scores, axis=2, keepdims=True)
    attn_probs = exp_scores / row_total
    log_total = row_peak[..., 0] + jnp.log(row_total[..., 0])
    attended = jnp.einsum(
        "hqk,khd->qhd",
        attn_probs.astype(jnp.bfloat16),
        vals_all,
        preferred_element_type=jnp.float32,
    )
    return (attended, log_total)


def attention_backward(queries, pair_all, log_total, attn_out, grad_attn, allowed):
    tok_rows, local_heads = (queries.shape[0], queries.shape[1])
    total_rows = pair_all.shape[0]
    local_width = local_heads * HD
    keys_all, vals_all = split_pairs(pair_all, local_heads)
    scale_factor = HD ** (-0.5)
    scores = (
        jnp.einsum("qhd,khd->hqk", queries, keys_all, preferred_element_type=jnp.float32)
        * scale_factor
    )
    scores = jnp.where(allowed[None], scores, MASKED)
    attn_probs = jnp.exp(scores - log_total[:, :, None])
    grad_heads = grad_attn.reshape(tok_rows, local_heads, HD)
    row_delta = jnp.sum(
        grad_heads.astype(jnp.float32)
        * attn_out.reshape(tok_rows, local_heads, HD).astype(jnp.float32),
        axis=2,
    )
    grad_probs = jnp.einsum(
        "qhd,khd->hqk", grad_heads, vals_all, preferred_element_type=jnp.float32
    )
    grad_scores = (attn_probs * (grad_probs - jnp.transpose(row_delta)[:, :, None])).astype(
        jnp.bfloat16
    )
    grad_query = (
        jnp.einsum("hqk,khd->qhd", grad_scores, keys_all, preferred_element_type=jnp.float32)
        * scale_factor
    )
    probs_rounded = attn_probs.astype(jnp.bfloat16)
    grad_keys = (
        jnp.einsum("hqk,qhd->khd", grad_scores, queries, preferred_element_type=jnp.float32)
        * scale_factor
    )
    grad_vals = jnp.einsum(
        "hqk,qhd->khd", probs_rounded, grad_heads, preferred_element_type=jnp.float32
    )
    key_terms = jnp.concatenate(
        [grad_keys.reshape(total_rows, local_width), grad_vals.reshape(total_rows, local_width)],
        axis=1,
    )
    own_rows = lax.psum_scatter(key_terms, CTX, scatter_dimension=0, tiled=True)
    return (
        grad_query,
        own_rows[:, :local_width].reshape(tok_rows, local_heads, HD),
        own_rows[:, local_width:],
    )


def layer_forward(hidden, weights, my_position, allowed):
    (
        norm1_gain,
        norm1_bias,
        norm2_gain,
        norm2_bias,
        qkv_w,
        qkv_b,
        dense_w,
        dense_b,
        up_w,
        up_b,
        down_w,
        down_b,
    ) = weights
    tok_rows = hidden.shape[0]
    local_width = qkv_w.shape[2]
    local_heads = local_width // HD
    hidden_wide = hidden.astype(jnp.float32)
    normed_one, scaled_one, inv_std_one = normalize(
        hidden_wide, norm1_gain.astype(jnp.float32), norm1_bias.astype(jnp.float32)
    )
    attn_input = normed_one.astype(jnp.bfloat16)
    mlp_input = (
        scaled_one * norm2_gain.astype(jnp.float32) + norm2_bias.astype(jnp.float32)
    ).astype(jnp.bfloat16)
    projected = (
        jnp.einsum("td,cde->cte", attn_input, qkv_w, preferred_element_type=jnp.float32)
        + qkv_b.astype(jnp.float32)[:, None, :]
    )
    cosine_table, sine_table = rotary_tables(my_position, ROT)
    queries = rotate(
        projected[0].reshape(tok_rows, local_heads, HD), cosine_table, sine_table, ROT
    ).astype(jnp.bfloat16)
    key_rows = rotate(
        projected[1].reshape(tok_rows, local_heads, HD), cosine_table, sine_table, ROT
    ).astype(jnp.bfloat16)
    value_rows = projected[2].astype(jnp.bfloat16)
    pair_local = jnp.concatenate([key_rows.reshape(tok_rows, local_width), value_rows], axis=1)
    pair_all = lax.all_gather(pair_local, CTX, axis=0, tiled=True)
    attended, log_total = attention_forward(queries, pair_all, allowed)
    attn_out = attended.reshape(tok_rows, local_width).astype(jnp.bfloat16)
    up_linear = jnp.dot(mlp_input, up_w, preferred_element_type=jnp.float32) + up_b.astype(
        jnp.float32
    )
    act_rounded = jax.nn.gelu(up_linear, approximate=False).astype(jnp.bfloat16)
    branch_terms = jnp.dot(attn_out, dense_w, preferred_element_type=jnp.float32) + jnp.dot(
        act_rounded, down_w, preferred_element_type=jnp.float32
    )
    summed = lax.psum(branch_terms, TEN)
    output = (
        hidden_wide + summed + dense_b.astype(jnp.float32) + down_b.astype(jnp.float32)
    ).astype(jnp.bfloat16)
    kept_state = (hidden, queries, pair_local, log_total, attn_out, up_linear, pair_all)
    return (output, kept_state)


def layer_backward(kept_state, cotangent, weights, my_position, allowed):
    (
        norm1_gain,
        norm1_bias,
        norm2_gain,
        norm2_bias,
        qkv_w,
        qkv_b,
        dense_w,
        dense_b,
        up_w,
        up_b,
        down_w,
        down_b,
    ) = weights
    hidden, queries, pair_local, log_total, attn_out, up_linear = (
        kept_state[0],
        kept_state[1],
        kept_state[2],
        kept_state[3],
        kept_state[4],
        kept_state[5],
    )
    pair_all = kept_state[6]
    tok_rows = hidden.shape[0]
    local_width = qkv_w.shape[2]
    hidden_wide = hidden.astype(jnp.float32)
    normed_one, scaled_one, inv_std_one = normalize(
        hidden_wide, norm1_gain.astype(jnp.float32), norm1_bias.astype(jnp.float32)
    )
    attn_input = normed_one.astype(jnp.bfloat16)
    mlp_input = (
        scaled_one * norm2_gain.astype(jnp.float32) + norm2_bias.astype(jnp.float32)
    ).astype(jnp.bfloat16)
    cot_wide = cotangent.astype(jnp.float32)
    act_rounded = jax.nn.gelu(up_linear, approximate=False).astype(jnp.bfloat16)
    grad_down_w = jnp.einsum(
        "tf,td->fd", act_rounded, cotangent, preferred_element_type=jnp.float32
    )
    grad_act = jnp.einsum("td,fd->tf", cotangent, down_w, preferred_element_type=jnp.float32)
    grad_up = grad_act * gelu_slope(up_linear)
    grad_up_bf = grad_up.astype(jnp.bfloat16)
    grad_up_w = jnp.einsum("td,tf->df", mlp_input, grad_up_bf, preferred_element_type=jnp.float32)
    grad_mlp = jnp.einsum("tf,df->td", grad_up_bf, up_w, preferred_element_type=jnp.float32)
    grad_dense_w = jnp.einsum("te,td->ed", attn_out, cotangent, preferred_element_type=jnp.float32)
    grad_attn = jnp.einsum(
        "td,ed->te", cotangent, dense_w, preferred_element_type=jnp.float32
    ).astype(jnp.bfloat16)
    grad_query, grad_keys, grad_vals = attention_backward(
        queries, pair_all, log_total, attn_out, grad_attn, allowed
    )
    cosine_table, sine_table = rotary_tables(my_position, ROT)
    grad_query = unrotate(grad_query, cosine_table, sine_table, ROT).reshape(tok_rows, local_width)
    grad_keys = unrotate(grad_keys, cosine_table, sine_table, ROT).reshape(tok_rows, local_width)
    grad_proj = jnp.stack([grad_query, grad_keys, grad_vals])
    grad_proj_bf = grad_proj.astype(jnp.bfloat16)
    grad_qkv_w = jnp.einsum(
        "td,cte->cde", attn_input, grad_proj_bf, preferred_element_type=jnp.float32
    )
    grad_attn_in = jnp.einsum(
        "cte,cde->td", grad_proj_bf, qkv_w, preferred_element_type=jnp.float32
    )
    grad_attn_in, grad_mlp = lax.psum((grad_attn_in, grad_mlp), TEN)
    grad_one, gain_one, shift_one = norm_backward(
        grad_attn_in, scaled_one, inv_std_one, norm1_gain.astype(jnp.float32)
    )
    grad_two, gain_two, shift_two = norm_backward(
        grad_mlp, scaled_one, inv_std_one, norm2_gain.astype(jnp.float32)
    )
    grad_hidden = (cot_wide + grad_one + grad_two).astype(jnp.bfloat16)
    bias_sum = jnp.sum(cot_wide, axis=0)
    qkv_bias_sum = jnp.sum(grad_proj, axis=1) * bias_keep(local_width)
    layer_grads = (
        gain_one,
        shift_one,
        gain_two,
        shift_two,
        grad_qkv_w,
        qkv_bias_sum,
        grad_dense_w,
        bias_sum,
        grad_up_w,
        jnp.sum(grad_up, axis=0),
        grad_down_w,
        bias_sum,
    )
    return (grad_hidden, layer_grads)


def body(
    layer_input,
    out_cotangent,
    seq_lengths,
    block_order,
    ln1_gain,
    ln1_bias,
    ln2_gain,
    ln2_bias,
    qkv_weight,
    qkv_bias,
    dense_weight,
    dense_bias,
    up_weight,
    up_bias,
    down_weight,
    down_bias,
):
    section_index = lax.axis_index(SEC)
    context_index = lax.axis_index(CTX)
    micro_count = layer_input.shape[0]
    tok_rows = layer_input.shape[1]
    block_rows = tok_rows // 2
    shards = (
        ln1_gain[0],
        ln1_bias[0],
        ln2_gain[0],
        ln2_bias[0],
        qkv_weight[0],
        qkv_bias[0],
        dense_weight[0],
        dense_bias[0],
        up_weight[0],
        up_bias[0],
        down_weight[0],
        down_bias[0],
    )
    forward_outs = []
    state_list = []
    incoming = jnp.zeros_like(layer_input[0])
    for tick_index in range(micro_count + 1):
        micro_index = jnp.clip(tick_index - section_index, 0, micro_count - 1)
        hidden = jnp.where(
            section_index == 0, layer_input[min(tick_index, micro_count - 1)], incoming
        )
        weights = gather_weights(shards)
        my_position, allowed, allowed_cols = micro_layout(
            seq_lengths, block_order, micro_index, block_rows, context_index, tok_rows
        )
        output, kept_state = layer_forward(hidden, weights, my_position, allowed)
        forward_outs.append(output)
        state_list.append(kept_state)
        if tick_index < micro_count:
            incoming = shifted(output, SEC, 1)
    stacked_outs = jnp.stack(forward_outs)
    layer_out = jnp.where(section_index == 0, stacked_outs[:micro_count], stacked_outs[1:])
    state_stack = jax.tree.map(lambda *leaves: jnp.stack(leaves), *state_list)
    grad_totals = None
    backward_outs = []
    incoming_grad = jnp.zeros_like(out_cotangent[0])
    for tick_index in range(micro_count + 1):
        micro_raw = tick_index - 1 + section_index
        is_valid = (micro_raw >= 0) & (micro_raw < micro_count)
        micro_index = jnp.clip(micro_raw, 0, micro_count - 1)
        state_index = jnp.clip(micro_raw + section_index, 0, micro_count)
        kept_state = jax.tree.map(
            lambda leaf_array: lax.dynamic_index_in_dim(leaf_array, state_index, 0, keepdims=False),
            state_stack,
        )
        cotangent = jnp.where(
            section_index == 1, out_cotangent[min(tick_index, micro_count - 1)], incoming_grad
        )
        weights = gather_weights(shards)
        my_position, allowed, allowed_cols = micro_layout(
            seq_lengths, block_order, micro_index, block_rows, context_index, tok_rows
        )
        grad_hidden, layer_grads = layer_backward(
            kept_state, cotangent, weights, my_position, allowed
        )
        layer_grads = jax.tree.map(
            lambda leaf_array: jnp.where(is_valid, leaf_array, 0.0), layer_grads
        )
        grad_totals = (
            layer_grads if grad_totals is None else jax.tree.map(jnp.add, grad_totals, layer_grads)
        )
        backward_outs.append(grad_hidden)
        if tick_index < micro_count:
            incoming_grad = shifted(grad_hidden, SEC, -1)
    stacked_grads = jnp.stack(backward_outs)
    input_grad = jnp.where(section_index == 1, stacked_grads[:micro_count], stacked_grads[1:])
    owned_grads = (
        lax.psum_scatter(
            grad_totals[0].astype(jnp.bfloat16), CTX, scatter_dimension=0, tiled=True
        ).astype(jnp.float32),
        lax.psum_scatter(
            grad_totals[1].astype(jnp.bfloat16), CTX, scatter_dimension=0, tiled=True
        ).astype(jnp.float32),
        lax.psum_scatter(
            grad_totals[2].astype(jnp.bfloat16), CTX, scatter_dimension=0, tiled=True
        ).astype(jnp.float32),
        lax.psum_scatter(
            grad_totals[3].astype(jnp.bfloat16), CTX, scatter_dimension=0, tiled=True
        ).astype(jnp.float32),
        lax.psum_scatter(
            grad_totals[4].astype(jnp.bfloat16), CTX, scatter_dimension=1, tiled=True
        ).astype(jnp.float32),
        lax.psum_scatter(
            grad_totals[5].astype(jnp.bfloat16), CTX, scatter_dimension=1, tiled=True
        ).astype(jnp.float32),
        lax.psum_scatter(
            grad_totals[6].astype(jnp.bfloat16), CTX, scatter_dimension=1, tiled=True
        ).astype(jnp.float32),
        lax.psum_scatter(
            grad_totals[7].astype(jnp.bfloat16), CTX, scatter_dimension=0, tiled=True
        ).astype(jnp.float32),
        lax.psum_scatter(
            grad_totals[8].astype(jnp.bfloat16), CTX, scatter_dimension=0, tiled=True
        ).astype(jnp.float32),
        lax.psum_scatter(
            grad_totals[9].astype(jnp.bfloat16), CTX, scatter_dimension=0, tiled=True
        ).astype(jnp.float32),
        lax.psum_scatter(
            grad_totals[10].astype(jnp.bfloat16), CTX, scatter_dimension=1, tiled=True
        ).astype(jnp.float32),
        lax.psum_scatter(
            grad_totals[11].astype(jnp.bfloat16), CTX, scatter_dimension=0, tiled=True
        ).astype(jnp.float32),
    )
    return (
        layer_out[None],
        input_grad[None],
        owned_grads[0][None],
        owned_grads[1][None],
        owned_grads[2][None],
        owned_grads[3][None],
        owned_grads[4][None],
        owned_grads[5][None],
        owned_grads[6][None],
        owned_grads[7][None],
        owned_grads[8][None],
        owned_grads[9][None],
        owned_grads[10][None],
        owned_grads[11][None],
    )


def wide_attention(queries, keys, vals, allowed):
    scores = jnp.einsum("qhd,khd->hqk", queries, keys, preferred_element_type=jnp.float32)
    scores = jnp.where(allowed[None], scores * HD ** (-0.5), MASKED)
    row_peak = jnp.max(scores, axis=2, keepdims=True)
    exp_scores = jnp.exp(scores - row_peak)
    probs = exp_scores / jnp.sum(exp_scores, axis=2, keepdims=True)
    attended = jnp.einsum(
        "hqk,khd->qhd", probs.astype(jnp.bfloat16), vals, preferred_element_type=jnp.float32
    )
    return (attended, probs)


def sum_kernel(sizes, backward, last, *refs):
    tensors, contexts = sizes
    count = tensors * contexts
    stride = next(i for i in range(tensors + 1, 2 * count) if math.gcd(i, count) == 1)
    refs = list(refs)
    parts = refs.pop(0)
    base = refs.pop(0)
    scaled, inv = (refs.pop(0), refs.pop(0)) if backward else (None, None)
    vec = refs.pop(0) if last else None
    out = refs.pop(0)
    vec_out = refs.pop(0) if last else None
    landed, send1, recv1, send2, recv2 = (refs.pop(0) for _ in range(5))
    vec_landed, vec_send, vec_recv = refs if last else (None, None, None)
    tensor = lax.axis_index(TEN)
    context = lax.axis_index(CTX)
    me = context * tensors + tensor

    def device(peer):
        return {TEN: lax.rem(peer, tensors), CTX: lax.div(peer, tensors)}

    def ahead(k):
        return lax.rem(me + k * stride, count)

    def behind(k):
        return lax.rem(me + (count - k) * stride, count)

    def copy_part(k, peer, slot):
        return pltpu.make_async_remote_copy(
            src_ref=parts.at[peer],
            dst_ref=landed.at[slot],
            send_sem=send1.at[k],
            recv_sem=recv1.at[slot],
            device_id=device(peer),
            device_id_type=pl.DeviceIdType.MESH,
        )

    def copy_vec(k, peer, slot):
        return pltpu.make_async_remote_copy(
            src_ref=vec.at[lax.div(peer, tensors)],
            dst_ref=vec_landed.at[slot],
            send_sem=vec_send.at[k],
            recv_sem=vec_recv.at[slot],
            device_id=device(peer),
            device_id_type=pl.DeviceIdType.MESH,
        )

    barrier = pltpu.get_barrier_semaphore()

    @pl.loop(1, count)
    def _(k):
        pl.semaphore_signal(
            barrier, inc=1, device_id=device(ahead(k)), device_id_type=pl.DeviceIdType.MESH
        )

    pl.semaphore_wait(barrier, count - 1)

    @pl.loop(1, count)
    def _(k):
        copy_part(k, ahead(k), me).start()
        if last:
            copy_vec(k, ahead(k), me).start()

    def add(k, total):
        source = behind(k)
        copy_part(k, source, source).wait_recv()
        return total + landed[source].astype(jnp.float32)

    total = lax.fori_loop(1, count, add, parts[me].astype(jnp.float32))
    if backward:
        xhat = scaled[...]
        total = inv[...] * (
            total
            - jnp.mean(total, axis=-1, keepdims=True)
            - xhat * jnp.mean(total * xhat, axis=-1, keepdims=True)
        )
    own_slot = tensor if last else me
    out[own_slot] = (base[...] + total).astype(out.dtype)
    members = tensors if last else count

    def copy_out(k, step, slot):
        if last:
            peer = context * tensors + lax.rem(tensor + step, tensors)
        else:
            peer = ahead(step)
        return pltpu.make_async_remote_copy(
            src_ref=out.at[own_slot],
            dst_ref=out.at[slot],
            send_sem=send2.at[k],
            recv_sem=recv2.at[slot],
            device_id=device(peer),
            device_id_type=pl.DeviceIdType.MESH,
        )

    @pl.loop(1, members)
    def _(k):
        copy_out(k, k, own_slot).start()

    if last:

        def add_vec(k, rows):
            source = behind(k)
            copy_vec(k, source, source).wait_recv()
            return rows + vec_landed[source]

        vec_out[...] = lax.fori_loop(1, count, add_vec, vec[context])

    @pl.loop(1, members)
    def _(k):
        slot = lax.rem(own_slot + members - k, members) if last else behind(k)
        copy_out(k, members - k, slot).wait_recv()

    @pl.loop(1, members)
    def _(k):
        copy_out(k, k, own_slot).wait_send()

    @pl.loop(1, count)
    def _(k):
        copy_part(k, ahead(k), me).wait_send()
        if last:
            copy_vec(k, ahead(k), me).wait_send()


def own_rows(x, rows):
    tensors = lax.axis_size(TEN)
    start = (lax.axis_index(CTX) * tensors + lax.axis_index(TEN)) * rows
    return lax.dynamic_slice_in_dim(x, start, rows, 0)


def sum_rows(parts, base, call_id, norm=(), vec=None):
    sizes = (lax.axis_size(TEN), lax.axis_size(CTX))
    count = sizes[0] * sizes[1]
    total_rows, features = parts.shape
    rows = total_rows // count
    last = vec is not None
    members = sizes[0] if last else count
    f32, bf16 = jnp.float32, jnp.bfloat16
    operands = [parts.astype(bf16).reshape(count, rows, features), own_rows(base, rows), *norm]
    outs = [jax.ShapeDtypeStruct((members, rows, features), bf16)]
    scratch = [pltpu.VMEM((count, rows, features), bf16)]
    scratch += [pltpu.SemaphoreType.DMA((count,))] * 4
    if last:
        operands.append(vec)
        outs.append(jax.ShapeDtypeStruct(vec.shape[1:], f32))
        scratch.append(pltpu.VMEM((count, *vec.shape[1:]), f32))
        scratch += [pltpu.SemaphoreType.DMA((count,))] * 2
    spec = pl.BlockSpec(memory_space=pltpu.VMEM)
    results = pl.pallas_call(
        functools.partial(sum_kernel, sizes, bool(norm), last),
        out_shape=outs,
        in_specs=[spec] * len(operands),
        out_specs=[spec] * len(outs),
        scratch_shapes=scratch,
        compiler_params=pltpu.CompilerParams(collective_id=call_id, has_side_effects=True),
    )(*operands)
    return (results[0].reshape(members * rows, features), *results[1:])


def wide_forward(hidden, weights, tables, allowed, call_id):
    gain1, bias1, gain2, bias2, dense_b, down_b, qkv_w, qkv_b, dense_w, up_w, up_b, down_w = weights
    rows = hidden.shape[0]
    width = qkv_w.shape[2]
    heads = width // HD
    hidden_wide = hidden.astype(jnp.float32)
    normed, scaled, inv_std = normalize(hidden_wide, gain1, bias1)
    attn_input = normed.astype(jnp.bfloat16)
    mlp_input = (scaled * gain2 + bias2).astype(jnp.bfloat16)
    projected = (
        jnp.einsum("td,cde->cte", attn_input, qkv_w, preferred_element_type=jnp.float32)
        + qkv_b[:, None, :]
    )
    queries = rotate(projected[0].reshape(rows, heads, HD), *tables, ROT).astype(jnp.bfloat16)
    keys = rotate(projected[1].reshape(rows, heads, HD), *tables, ROT).astype(jnp.bfloat16)
    vals = projected[2].astype(jnp.bfloat16).reshape(rows, heads, HD)
    attended, probs = wide_attention(queries, keys, vals, allowed)
    attn_out = attended.reshape(rows, width).astype(jnp.bfloat16)
    up_linear = jnp.dot(mlp_input, up_w, preferred_element_type=jnp.float32) + up_b
    act = jax.nn.gelu(up_linear, approximate=False).astype(jnp.bfloat16)
    parts = jnp.dot(attn_out, dense_w, preferred_element_type=jnp.float32) + jnp.dot(
        act, down_w, preferred_element_type=jnp.float32
    )
    (output,) = sum_rows(parts, hidden_wide + (dense_b + down_b), call_id)
    state = (attn_input, mlp_input, scaled, inv_std, queries, keys, vals, probs, attn_out, up_linear, act)
    return (output, state)


def wide_backward(state, cotangent, weights, tables, call_id, later):
    gain1, bias1, gain2, bias2, dense_b, down_b, qkv_w, qkv_b, dense_w, up_w, up_b, down_w = weights
    attn_input, mlp_input, scaled, inv_std, queries, keys, vals, probs, attn_out, up_linear, act = state
    rows = cotangent.shape[0]
    width = qkv_w.shape[2]
    heads = width // HD
    f32 = jnp.float32
    cot_wide = cotangent.astype(f32)
    grad_act = jnp.einsum("td,fd->tf", cotangent, down_w, preferred_element_type=f32)
    grad_up = grad_act * gelu_slope(up_linear)
    grad_up_bf = grad_up.astype(jnp.bfloat16)
    grad_attn = jnp.einsum("td,ed->te", cotangent, dense_w, preferred_element_type=f32).astype(
        jnp.bfloat16
    )
    grad_heads = grad_attn.reshape(rows, heads, HD)
    delta = jnp.sum(
        grad_heads.astype(f32) * attn_out.reshape(rows, heads, HD).astype(f32), axis=2
    )
    grad_probs = jnp.einsum("qhd,khd->hqk", grad_heads, vals, preferred_element_type=f32)
    grad_scores = (probs * (grad_probs - jnp.transpose(delta)[:, :, None])).astype(jnp.bfloat16)
    scale = HD ** (-0.5)
    grad_q = jnp.einsum("hqk,khd->qhd", grad_scores, keys, preferred_element_type=f32) * scale
    grad_k = jnp.einsum("hqk,qhd->khd", grad_scores, queries, preferred_element_type=f32) * scale
    grad_v = jnp.einsum(
        "hqk,qhd->khd", probs.astype(jnp.bfloat16), grad_heads, preferred_element_type=f32
    )
    grad_proj = jnp.stack(
        [
            unrotate(grad_q, *tables, ROT).reshape(rows, width),
            unrotate(grad_k, *tables, ROT).reshape(rows, width),
            grad_v.reshape(rows, width),
        ]
    )
    grad_proj_bf = grad_proj.astype(jnp.bfloat16)
    grad_a1 = jnp.einsum("cte,cde->td", grad_proj_bf, qkv_w, preferred_element_type=f32)
    grad_a2 = jnp.einsum("tf,df->td", grad_up_bf, up_w, preferred_element_type=f32)
    shared = jnp.stack(
        [
            jnp.sum(grad_a1 * scaled, axis=0),
            jnp.sum(grad_a1, axis=0),
            jnp.sum(grad_a2 * scaled, axis=0),
            jnp.sum(grad_a2, axis=0),
        ]
    )
    first = (lax.axis_index(TEN) == 0) & (lax.axis_index(CTX) == 0)
    bias_sum = jnp.where(first, jnp.sum(cot_wide, axis=0), 0.0)
    shared = jnp.concatenate([shared, bias_sum[None]], axis=0)
    own = jnp.concatenate(
        [
            (jnp.sum(grad_proj, axis=1) * bias_keep(width)).reshape(-1),
            jnp.sum(grad_up, axis=0),
        ]
    )
    grad_w = (
        jnp.einsum("td,cte->cde", attn_input, grad_proj_bf, preferred_element_type=f32),
        jnp.einsum("te,td->ed", attn_out, cotangent, preferred_element_type=f32),
        jnp.einsum("td,tf->df", mlp_input, grad_up_bf, preferred_element_type=f32),
        jnp.einsum("tf,td->fd", act, cotangent, preferred_element_type=f32),
    )
    rows = rows // (lax.axis_size(TEN) * lax.axis_size(CTX))
    xhat = own_rows(scaled, rows)
    norm = (xhat, jnp.broadcast_to(own_rows(inv_std, rows), xhat.shape))
    vec = None
    if later is not None:
        vec = jnp.concatenate([shared, later, jnp.zeros((6, shared.shape[1]), f32)], axis=0)
        vec = vec.reshape(vec.shape[0], lax.axis_size(CTX), -1).swapaxes(0, 1)
    grad_hidden, *rest = sum_rows(
        grad_a1 * gain1 + grad_a2 * gain2, cot_wide, call_id, norm, vec
    )
    return (grad_hidden, rest[0] if rest else shared, own, grad_w)


def swap_sections(pair):
    section = lax.axis_index(SEC)
    theirs = lax.dynamic_index_in_dim(pair, 1 - section, 0, keepdims=False)
    mine = lax.dynamic_index_in_dim(pair, section, 0, keepdims=False)
    return (mine, lax.ppermute(theirs, SEC, [(0, 1), (1, 0)]))


def wide_body(
    layer_input,
    out_cotangent,
    seq_lengths,
    block_order,
    ln1_gain,
    ln1_bias,
    ln2_gain,
    ln2_bias,
    qkv_weight,
    qkv_bias,
    dense_weight,
    dense_bias,
    up_weight,
    up_bias,
    down_weight,
    down_bias,
):
    f32 = jnp.float32
    bf16 = jnp.bfloat16
    section = lax.axis_index(SEC)
    context = lax.axis_index(CTX)
    tok_rows = layer_input.shape[1]
    block_rows = tok_rows * lax.axis_size(CTX) // block_order.shape[1]
    edges = jnp.stack(
        [
            lax.dynamic_index_in_dim(layer_input, section, 0, keepdims=False),
            lax.dynamic_index_in_dim(out_cotangent, section, 0, keepdims=False),
        ]
    )
    edges = lax.all_gather(edges, CTX, axis=1, tiled=True)
    vectors = jnp.concatenate([ln1_gain, ln1_bias, ln2_gain, ln2_bias, dense_bias, down_bias], axis=0)
    vectors = lax.all_gather(
        lax.all_gather(vectors, CTX, axis=1, tiled=True), SEC, axis=0
    ).astype(f32)
    own_bias = lax.all_gather(
        jnp.concatenate([qkv_bias[0].reshape(-1), up_bias[0]]), SEC, axis=0
    ).astype(f32)
    width = qkv_bias.shape[2]
    matrices = (
        lax.all_to_all(qkv_weight[0], CTX, 2, 1, tiled=True),
        lax.all_to_all(dense_weight[0], CTX, 0, 1, tiled=True),
        lax.all_to_all(up_weight[0], CTX, 1, 0, tiled=True),
        lax.all_to_all(down_weight[0], CTX, 0, 1, tiled=True),
    )
    matrices = tuple(lax.all_gather(leaf, SEC, axis=0) for leaf in matrices)
    weights = [
        (
            *(vectors[layer, i] for i in range(6)),
            matrices[0][layer],
            own_bias[layer, : 3 * width].reshape(3, width),
            matrices[1][layer],
            matrices[2][layer],
            own_bias[layer, 3 * width :],
            matrices[3][layer],
        )
        for layer in range(2)
    ]
    lengths = lax.dynamic_index_in_dim(seq_lengths, section, 0, keepdims=False)
    perm = lax.dynamic_index_in_dim(block_order, section, 0, keepdims=False)
    packed_pos, segment_id, position = packed_layout(lengths, perm, block_rows)
    allowed = (segment_id[:, None] == segment_id[None, :]) & (
        packed_pos[None, :] <= packed_pos[:, None]
    )
    tables = rotary_tables(position, ROT)
    hidden = edges[0]
    states = []
    outs = []
    for layer in range(2):
        hidden, state = wide_forward(hidden, weights[layer], tables, allowed, layer)
        outs.append(hidden)
        states.append(state)
    cotangent = edges[1]
    grads = [None, None]
    cots = [None, None]
    for layer in (1, 0):
        cotangent, shared, own, grad_w = wide_backward(
            states[layer],
            cotangent,
            weights[layer],
            tables,
            2 + layer,
            None if layer else grads[1][0],
        )
        cots[layer] = cotangent
        grads[layer] = (shared, own, grad_w)
    local = [
        lax.dynamic_slice_in_dim(rows, context * tok_rows, tok_rows, 0)
        for rows in (outs[0], outs[1], cots[1])
    ]
    both = jnp.stack([jnp.stack([local[0], cots[0]]), jnp.stack([local[1], local[2]])])
    mine, theirs = swap_sections(both)
    low = jnp.where(section == 0, mine, theirs)
    high = jnp.where(section == 0, theirs, mine)
    layer_out = jnp.stack([low[0], high[0]])
    input_grad = jnp.stack([low[1], high[1]])
    vec = grads[0][0][:10].reshape(2, -1)
    own = jnp.stack([grads[0][1], grads[1][1]])
    mine, theirs = swap_sections(jnp.concatenate([vec, own], axis=1))
    own = mine + theirs
    shared = own[: vec.shape[1]].reshape(5, -1)
    own = own[vec.shape[1] :]
    summed = []
    for i in range(4):
        pair = jnp.stack([grads[0][2][i], grads[1][2][i]])
        mine = lax.dynamic_index_in_dim(pair, section, 0, keepdims=False)
        theirs = lax.dynamic_index_in_dim(pair, 1 - section, 0, keepdims=False).astype(bf16)
        summed.append(
            (mine + lax.ppermute(theirs, SEC, [(0, 1), (1, 0)]).astype(f32)).astype(bf16)
        )
    qkv_g = lax.all_to_all(summed[0], CTX, 1, 2, tiled=True).astype(f32)
    dense_g = lax.all_to_all(summed[1], CTX, 1, 0, tiled=True).astype(f32)
    up_g = lax.all_to_all(summed[2], CTX, 0, 1, tiled=True).astype(f32)
    down_g = lax.all_to_all(summed[3], CTX, 1, 0, tiled=True).astype(f32)
    return (
        layer_out[None],
        input_grad[None],
        shared[0][None],
        shared[1][None],
        shared[2][None],
        shared[3][None],
        qkv_g[None],
        own[: 3 * width].reshape(1, 3, width),
        dense_g[None],
        shared[4][None],
        up_g[None],
        own[3 * width :][None],
        down_g[None],
        shared[4][None],
    )


def plan(*args):
    heads = args[10].shape[1] // HD
    units = lax.axis_size(CTX)
    count = units * lax.axis_size(TEN)
    tiled = args[0].shape[1] * units % (16 * count) == 0
    if heads % units == 0 and tiled and args[0].shape[0] == lax.axis_size(SEC) == 2:
        return wide_body(*args)
    return body(*args)


def solution(mesh):
    return jax.shard_map(
        plan,
        mesh=mesh,
        in_specs=(
            P(None, CTX, None),
            P(None, CTX, None),
            P(),
            P(),
            P(SEC, CTX),
            P(SEC, CTX),
            P(SEC, CTX),
            P(SEC, CTX),
            P(SEC, None, CTX, TEN),
            P(SEC, None, (TEN, CTX)),
            P(SEC, TEN, CTX),
            P(SEC, CTX),
            P(SEC, CTX, TEN),
            P(SEC, (TEN, CTX)),
            P(SEC, TEN, CTX),
            P(SEC, CTX),
        ),
        out_specs=(
            P(SEC, None, CTX, None),
            P(SEC, None, CTX, None),
            P(SEC, CTX),
            P(SEC, CTX),
            P(SEC, CTX),
            P(SEC, CTX),
            P(SEC, None, CTX, TEN),
            P(SEC, None, (TEN, CTX)),
            P(SEC, TEN, CTX),
            P(SEC, CTX),
            P(SEC, CTX, TEN),
            P(SEC, (TEN, CTX)),
            P(SEC, TEN, CTX),
            P(SEC, CTX),
        ),
        check_vma=False,
    )
```
